256 devices in a mesh: shot: 32 (over z, y_hi, core), ap: 8 (over x, y_lo).
Axes of the slice: x: 4, y: 4 (y_hi: 2, y_lo: 2; y = y_hi * 2 + y_lo), z: 8, core: 2. Of those that a mesh axis runs over, the one named last changes fastest.
Arguments:
- velocity_tiles: float32 [512, 64, 1024], P('shot', 'ap'), may hold values from 1.5 to 4.5
- aperture_tiles: int32 [32, 16], replicated, may hold values from 0 to 511, as said below
- source_cells: int32 [32], P('shot'), may hold values from 0 to 1048575
- wavelet: float32 [32, 6], P('shot'), may hold values from -48 to 48
- receiver_cells: int32 [32, 256], P('shot'), may hold values from 0 to 1048575
- observed: float32 [32, 6, 256], P('shot'), may hold values from -24 to 24
- field_early: float32 [32, 64, 128, 128], P('shot', 'ap'), may hold values from -6 to 6
- field_late: float32 [32, 64, 128, 128], P('shot', 'ap'), may hold values from -6 to 6
- adjoint_late: float32 [32, 64, 128, 128], P('shot', 'ap'), may hold values from -6 to 6
- adjoint_later: float32 [32, 64, 128, 128], P('shot', 'ap'), may hold values from -6 to 6
Outputs:
- grad_tiles: float32 [512, 64, 1024], P('shot', 'ap')
The draws below stay inside these ranges and needn't reach their ends.
Inputs may be any that keep to these rules, and one draw needn't show every extreme that they name: `aperture_tiles`: the 16 tiles of one shot belong to 16 different owners, tile t being owned by index t // 16 of shot; some owners appear in far more shots than others.
All inputs are finite; a program needn't handle non-finite values.
Results may differ from the reference program's by a relative error of at most 0.0003.
Values sent between devices are 32-bit elements; how exact they have to be, the bound alone decides.
A program may use at most 64 MiB of HBM per device.

```python
import jax
import jax.numpy as jnp
from jax import lax

TILE = 32
GA = 4
NT = 6
NREC = 256
TILES_DEV = 16
SHOTS = 32
TILES = 512
DEPTH = 64
AX = 128


def draw_aperture_tiles(key, part):
    order_key, score_key, local_key = jax.random.split(key, 3)
    hot_count = max(1, GA * GA // 4)
    ranking = jax.random.permutation(order_key, SHOTS)
    hotness = jnp.zeros((SHOTS,), jnp.int32).at[ranking[:hot_count]].set(1)
    scores = jax.random.randint(score_key, (SHOTS, SHOTS), 0, 1024) + 4096 * hotness[None, :]
    scores = scores * SHOTS + jnp.arange(SHOTS, dtype=jnp.int32)[None, :]
    chosen = lax.top_k(scores, GA * GA)[1].astype(jnp.int32)
    local_pick = jax.random.randint(local_key, (SHOTS, GA * GA), 0, TILES_DEV)
    return (chosen * TILES_DEV + local_pick).astype(jnp.int32)


def touch_ends(drawn, key, smallest, top_value):
    extent = drawn.shape
    spot = [jax.random.randint(jax.random.fold_in(key, axis), (), 0, extent[axis]) for axis in range(len(extent))]
    drawn = drawn.at[tuple(spot)].set(smallest)
    longest = extent.index(max(extent))
    spot[longest] = (spot[longest] + 1) % extent[longest]
    return drawn.at[tuple(spot)].set(top_value)


def block_scale(rng, shape, cuts, least, largest):
    def one(axis_at, shards_of):
        draws = jax.random.uniform(jax.random.fold_in(jax.random.fold_in(rng, 6), axis_at), (shards_of,), jnp.float32, least / len(cuts), largest / len(cuts))
        return jnp.repeat(jnp.exp(draws), shape[axis_at] // shards_of).reshape((-1,) + (1,) * (len(shape) - axis_at - 1))

    loudness = one(*cuts[0])
    for cut in cuts[1:]:
        loudness = loudness * one(*cut)
    return loudness


def gaussian(own_key, shape, deviation, reach, cuts=(), kind=jnp.bfloat16):
    drawn = jax.random.normal(own_key, shape, jnp.float32) * deviation
    if len(cuts) > 0:
        drawn = block_scale(own_key, shape, cuts, -0.22, 0.18) * drawn
    return jnp.clip(drawn, min=-reach, max=reach).astype(kind)


def setup_inputs(seed: int = 0) -> dict:
    splits = jax.random.split(jax.random.key(seed), 11)
    return {
        "velocity_tiles": jnp.clip(1.5 + 3.0 * jax.random.uniform(splits[0], (TILES, DEPTH, TILE * TILE), jnp.float32) ** block_scale(splits[0], (TILES, DEPTH, TILE * TILE), ((0, 32), (1, 8)), -0.2, 0.2), 1.5, 4.5),
        "aperture_tiles": draw_aperture_tiles(jax.random.fold_in(splits[10], 71), 0),
        "source_cells": touch_ends(jax.random.randint(splits[2], (SHOTS,), 0, DEPTH * AX * AX), jax.random.fold_in(splits[2], 1), 0, (DEPTH * AX * AX) - 1).astype(jnp.int32),
        "wavelet": gaussian(splits[3], (SHOTS, NT), 8.0, 48.0, ((0, 32),), jnp.float32),
        "receiver_cells": touch_ends(jax.random.randint(splits[4], (SHOTS, NREC), 0, DEPTH * AX * AX), jax.random.fold_in(splits[4], 1), 0, (DEPTH * AX * AX) - 1).astype(jnp.int32),
        "observed": gaussian(splits[5], (SHOTS, NT, NREC), 4.0, 24.0, ((0, 32),), jnp.float32),
        "field_early": gaussian(splits[6], (SHOTS, DEPTH, AX, AX), 1.0, 6.0, ((0, 32), (1, 8)), jnp.float32),
        "field_late": gaussian(splits[7], (SHOTS, DEPTH, AX, AX), 1.0, 6.0, ((0, 32), (1, 8)), jnp.float32),
        "adjoint_late": gaussian(splits[8], (SHOTS, DEPTH, AX, AX), 1.0, 6.0, ((0, 32), (1, 8)), jnp.float32),
        "adjoint_later": gaussian(splits[9], (SHOTS, DEPTH, AX, AX), 1.0, 6.0, ((0, 32), (1, 8)), jnp.float32),
    }


COEF = (-205.0 / 72.0, 8.0 / 5.0, -1.0 / 5.0, 8.0 / 315.0, -1.0 / 560.0)
STEP_SQUARE = 0.01


def stencil(padded):
    row_count = padded.shape[0] - 8
    width_x = padded.shape[1]
    width_y = padded.shape[2]
    widened = jnp.pad(padded, ((0, 0), (4, 4), (4, 4)))
    centre = widened[4:4 + row_count, 4:4 + width_x, 4:4 + width_y]
    result = (3.0 * COEF[0]) * centre
    for k in range(1, 5):
        beside = widened[4 + k:4 + k + row_count, 4:4 + width_x, 4:4 + width_y] + widened[4 - k:4 - k + row_count, 4:4 + width_x, 4:4 + width_y]
        beside = beside + widened[4:4 + row_count, 4 + k:4 + k + width_x, 4:4 + width_y] + widened[4:4 + row_count, 4 - k:4 - k + width_x, 4:4 + width_y]
        beside = beside + widened[4:4 + row_count, 4:4 + width_x, 4 + k:4 + k + width_y] + widened[4:4 + row_count, 4:4 + width_x, 4 - k:4 - k + width_y]
        result = result + COEF[k] * beside
    return result


def advance(previous, padded_current, coef_field, inject):
    update = coef_field * (stencil(padded_current) + inject)
    return 2.0 * padded_current[4:-4] - previous + update, update


def deposit(row_count, first_row, width_x, width_y, cell_index, values):
    plane_cells = width_x * width_y
    flat_index = cell_index - first_row * plane_cells
    inside = (flat_index >= 0) & (flat_index < row_count * plane_cells)
    flat_index = jnp.where(inside, flat_index, row_count * plane_cells).astype(jnp.int32)
    deposited = jnp.zeros((row_count * plane_cells,), jnp.float32).at[flat_index].add(values.astype(jnp.float32), mode="drop")
    return deposited.reshape(row_count, width_x, width_y)


def assemble(pieces, tile_grid, tile_edge):
    row_count = pieces.shape[1]
    blocks = pieces.reshape(tile_grid, tile_grid, row_count, tile_edge, tile_edge)
    return blocks.transpose(2, 0, 3, 1, 4).reshape(row_count, tile_grid * tile_edge, tile_grid * tile_edge)


def dissect(whole, tile_grid, tile_edge):
    row_count = whole.shape[0]
    blocks = whole.reshape(row_count, tile_grid, tile_edge, tile_grid, tile_edge)
    return blocks.transpose(1, 3, 0, 2, 4).reshape(tile_grid * tile_grid, row_count, tile_edge * tile_edge)


def depth_pad(whole):
    return jnp.pad(whole, ((4, 4), (0, 0), (0, 0)))


def reference(velocity_tiles, aperture_tiles, source_cells, wavelet, receiver_cells, observed, field_early, field_late, adjoint_late, adjoint_later):
    def one_shot(packed):
        tile_ids, source_cell, wavelet_row, receivers, recorded, early, late, adjoint_now, adjoint_next = packed
        velocity = assemble(velocity_tiles[tile_ids], GA, TILE)
        courant_sq = STEP_SQUARE * velocity * velocity
        previous, current = early, late
        updates = []
        traces = []
        for moment in range(NT):
            inject = deposit(DEPTH, 0, AX, AX, source_cell[None], wavelet_row[moment][None])
            advanced, update = advance(previous, depth_pad(current), courant_sq, inject)
            updates.append(update)
            traces.append(advanced.reshape(-1)[receivers])
            previous, current = current, advanced
        residual = jnp.stack(traces) - recorded
        image_sum = jnp.zeros_like(velocity)
        for moment in reversed(range(NT)):
            inject = deposit(DEPTH, 0, AX, AX, receivers, residual[moment])
            adjoint_new, unused = advance(adjoint_next, depth_pad(adjoint_now), courant_sq, inject)
            image_sum = image_sum + adjoint_new * updates[moment]
            adjoint_next, adjoint_now = adjoint_now, adjoint_new
        gradient = 2.0 * image_sum / velocity
        return dissect(gradient, GA, TILE)

    per_shot = lax.map(one_shot, (aperture_tiles, source_cells, wavelet, receiver_cells, observed, field_early, field_late, adjoint_late, adjoint_later))
    grad_tiles = jnp.zeros(velocity_tiles.shape, jnp.float32)
    grad_tiles = grad_tiles.at[aperture_tiles.reshape(-1)].add(per_shot.reshape(-1, DEPTH, TILE * TILE))
    return grad_tiles
```

```python
import functools

import jax
import jax.numpy as jnp
from jax import lax
from jax.experimental import pallas as pl
from jax.experimental.pallas import tpu as pltpu
from jax.sharding import PartitionSpec as P

COEF = (-205.0 / 72.0, 8.0 / 5.0, -1.0 / 5.0, 8.0 / 315.0, -1.0 / 560.0)
STEP_SQUARE = 0.01
MESH = pl.DeviceIdType.MESH
STEPS = 6
F32 = jnp.float32
BF16 = jnp.bfloat16
Z_ORDER = (4, 3, 5, 2, 6, 1, 7, 0)


def ap_of(half, quarter):
    mirror = quarter // 2
    y = ((quarter + 1) // 2) % 2
    x = mirror + half * (1 - 2 * mirror)
    return 4 * half + 2 * x + y


def split(value):
    high = value.astype(BF16)
    return high, (value - high.astype(F32)).astype(BF16)


def kernel(
    meta, wav, cells, observed, vel, early, late, a_late, a_later, out,
    fwd, adj, upd, inj, coef, count, image, lap, turn, ymat, hot,
    xs, xr, vsend, vrecv, vpiece, vtile, gtile, gpiece, gsend, grecv,
    f_send, f_recv, f_loc, z_send, z_recv, x_send, x_recv,
    v_send, v_recv, g_send, g_recv, t_send, t_recv, p_send, p_recv,
):
    shots = lax.axis_size("shot")
    me = lax.axis_index("shot")
    ap = lax.axis_index("ap")
    half = ap // 4
    slab = ap % 4
    xl = slab // 2
    yl = slab % 2
    mirror = xl + half * (1 - 2 * xl)
    quarter = yl + mirror * (3 - 2 * yl)
    has_low = quarter > 0
    has_high = quarter < 3

    @pl.loop(1, 7)
    def _(n):
        for buf in (fwd, adj):
            buf[n, 0:4, 8:40, :] = jnp.zeros((4, 32, 128), F32)
            buf[n, 36:40, 8:40, :] = jnp.zeros((4, 32, 128), F32)

    fields = ((late, fwd, 1), (early, fwd, 0), (a_late, adj, 6), (a_later, adj, 7))

    def own_copy(f):
        source, buf, n = fields[f]
        return pltpu.make_async_copy(
            source.at[0, :, pl.ds(32 * quarter, 32), :],
            buf.at[n, pl.ds(4 + 8 * slab, 8), pl.ds(8, 32), :],
            f_loc.at[f],
        )

    def field_copy(f, i):
        source, buf, n = fields[f]
        other = (quarter + i) % 4
        return pltpu.make_async_remote_copy(
            src_ref=source.at[0, :, pl.ds(32 * other, 32), :],
            dst_ref=buf.at[n, pl.ds(4 + 8 * slab, 8), pl.ds(8, 32), :],
            send_sem=f_send.at[f, i - 1],
            recv_sem=f_recv.at[f, i - 1],
            device_id={"ap": ap_of(half, other)},
            device_id_type=MESH,
        )

    for f in range(4):
        own_copy(f).start()

    barrier = pltpu.get_barrier_semaphore()

    @pl.loop(1, shots)
    def _(d):
        pl.semaphore_signal(
            barrier, inc=1, device_id={"shot": (me + d) % shots}, device_id_type=MESH
        )

    for i in range(1, 4):
        pl.semaphore_signal(
            barrier, inc=1, device_id={"ap": ap_of(half, (quarter + i) % 4)}, device_id_type=MESH
        )
    partner = ap_of(1 - half, quarter)
    pl.semaphore_signal(barrier, inc=1, device_id={"ap": partner}, device_id_type=MESH)

    @pl.loop(0, shots)
    def _(s):
        vsend[s] = vel[meta[s]]

    vrecv[me] = vel[meta[me]]

    pl.semaphore_wait(barrier, shots - 1 + 4)

    for f in (0, 1):
        for i in range(1, 4):
            field_copy(f, i).start()

    def exchange_copy(src, dst, target, send, recv):
        return pltpu.make_async_remote_copy(
            src_ref=src.at[target],
            dst_ref=dst.at[me],
            send_sem=send.at[target],
            recv_sem=recv.at[me],
            device_id={"shot": target},
            device_id_type=MESH,
        )

    def arrival(src, dst, origin, send, recv):
        return pltpu.make_async_remote_copy(
            src_ref=src.at[origin],
            dst_ref=dst.at[origin],
            send_sem=send.at[origin],
            recv_sem=recv.at[origin],
            device_id={"shot": origin},
            device_id_type=MESH,
        )

    def exchange_start(src, dst, send, recv):
        planes = shots // 4
        for core in range(2):
            for dz in range(planes):
                for dy in range(2):
                    step = Z_ORDER[dz] if planes == 8 else dz
                    target = (
                        ((me // 4 + step) % planes) * 4 + ((me // 2 + dy) % 2) * 2 + core
                    )

                    @pl.when(target != me)
                    def _():
                        exchange_copy(src, dst, target, send, recv).start()

    exchange_start(vsend, vrecv, v_send, v_recv)

    for f in (2, 3):
        for i in range(1, 4):
            field_copy(f, i).start()

    distance = jnp.abs(
        lax.broadcasted_iota(jnp.int32, (128, 128), 0)
        - lax.broadcasted_iota(jnp.int32, (128, 128), 1)
    )
    band = jnp.where(distance == 0, 3.0 * COEF[0], 0.0)
    for k in range(1, 5):
        band = jnp.where(distance == k, COEF[k], band)
    band_high, band_low = split(band)
    ymat[0:128, 0:128] = band_high
    ymat[128:256, 0:128] = band_high
    ymat[0:128, 128:256] = band_low
    ymat[128:256, 128:256] = jnp.zeros((128, 128), BF16)

    @pl.loop(1, 7)
    def _(n):
        @pl.loop(0, 8)
        def _(g):
            for buf in (fwd, adj):
                buf[n, pl.ds(4 + 4 * g, 4), 0:8, :] = jnp.zeros((4, 8, 128), F32)
                buf[n, pl.ds(4 + 4 * g, 4), 40:48, :] = jnp.zeros((4, 8, 128), F32)

    flat = cells[0:1, :]
    z_at = flat // 16384 - 32 * half
    x_at = (flat // 128) % 128 - 32 * quarter
    y_at = flat % 128
    inside = (z_at >= 0) & (z_at < 32) & (x_at >= 0) & (x_at < 32)
    row_at = jnp.where(inside, z_at * 32 + x_at, -1)
    nrec = cells.shape[1]

    @pl.loop(0, 16)
    def _(b):
        rows = lax.broadcasted_iota(jnp.int32, (64, nrec), 0) + b * 64
        hot[pl.ds(b * 64, 64), :] = jnp.where(rows == row_at, 1.0, 0.0).astype(BF16)

    lanes = jnp.where(
        lax.broadcasted_iota(jnp.int32, (128, nrec), 0) == y_at, 1.0, 0.0
    )
    contract = (((1,), (1,)), ((), ()))
    lanes_low = lanes.astype(BF16)

    @pl.loop(0, 4)
    def _(b):
        found = lax.dot_general(
            hot[pl.ds(b * 256, 256), :], lanes_low, contract, preferred_element_type=F32
        )
        count[pl.ds(8 * b, 8), :, :] = found.reshape(8, 32, 128)

    for n in range(STEPS):
        high, low = split(lanes * observed[0, n : n + 1, :])
        both = jnp.concatenate([high, low], axis=0)

        @pl.loop(0, 4)
        def _(b):
            found = lax.dot_general(
                hot[pl.ds(b * 256, 256), :], both, contract, preferred_element_type=F32
            )
            inj[n, pl.ds(8 * b, 8), :, :] = (found[:, 0:128] + found[:, 128:256]).reshape(
                8, 32, 128
            )

    def z_copy(buf, n, e):
        return pltpu.make_async_remote_copy(
            src_ref=buf.at[n, pl.ds(32 - 28 * half, 4), pl.ds(8, 32), :],
            dst_ref=buf.at[n, pl.ds(36 * half, 4), pl.ds(8, 32), :],
            send_sem=z_send.at[e],
            recv_sem=z_recv.at[e],
            device_id={"ap": partner},
            device_id_type=MESH,
        )

    def x_copy(e, side, c):
        other = ap_of(half, quarter + (2 * side - 1))
        return pltpu.make_async_remote_copy(
            src_ref=xs.at[e, side, pl.ds(8 * c, 8)],
            dst_ref=xr.at[e, 1 - side, pl.ds(8 * c, 8)],
            send_sem=x_send.at[e, side, c],
            recv_sem=x_recv.at[e, 1 - side, c],
            device_id={"ap": other},
            device_id_type=MESH,
        )

    def x_arrival(e, side, c):
        other = ap_of(half, quarter + (2 * side - 1))
        return pltpu.make_async_remote_copy(
            src_ref=xs.at[e, side, pl.ds(8 * c, 8)],
            dst_ref=xr.at[e, side, pl.ds(8 * c, 8)],
            send_sem=x_send.at[e, side, c],
            recv_sem=x_recv.at[e, side, c],
            device_id={"ap": other},
            device_id_type=MESH,
        )

    def x_post(buf, n, e, c):
        at = pl.ds(4 + 8 * c, 8)

        @pl.when(has_low)
        def _():
            xs[e, 0, pl.ds(8 * c, 8)] = buf[n, at, 8:12, :]
            x_copy(e, 0, c).start()

        @pl.when(has_high)
        def _():
            xs[e, 1, pl.ds(8 * c, 8)] = buf[n, at, 36:40, :]
            x_copy(e, 1, c).start()

    def x_take(buf, n, e, c):
        at = pl.ds(4 + 8 * c, 8)

        @pl.when(has_low)
        def _():
            x_arrival(e, 0, c).wait_recv()
            buf[n, at, 4:8, :] = xr[e, 0, pl.ds(8 * c, 8)]

        @pl.when(has_high)
        def _():
            x_arrival(e, 1, c).wait_recv()
            buf[n, at, 40:44, :] = xr[e, 1, pl.ds(8 * c, 8)]

    def chunk_at(i):
        return i * half + (3 - i) * (1 - half)

    def fields_ready(f):
        own_copy(f).wait()
        for i in range(1, 4):
            field_copy(f, i).wait_recv()

    def lateral(buf, n):
        @pl.loop(0, 4)
        def _(c):
            here = buf[n, pl.ds(4 + 8 * c, 8), 8:40, :].reshape(256, 128)
            both = jnp.concatenate(split(here), axis=1)
            found = jnp.dot(both, ymat[...], preferred_element_type=F32)
            lap[pl.ds(8 * c, 8), :, :] = (found[:, 0:128] + found[:, 128:256]).reshape(8, 32, 128)

    for f, e in ((0, 0), (2, 6)):
        buf, n = fields[f][1:]
        fields_ready(f)
        z_copy(buf, n, e).start()
        for i in range(4):
            x_post(buf, n, e, chunk_at(i))
    fields_ready(1)
    fields_ready(3)
    lateral(fwd, 1)

    @pl.loop(0, shots)
    def _(s):
        @pl.when(s != me)
        def _():
            arrival(vsend, vrecv, s, v_send, v_recv).wait_recv()

    @pl.loop(0, 16)
    def _(k):
        vpiece[k] = vrecv[meta[2 * shots + k]]

    def tile_copy(i):
        other = (quarter + i) % 4
        return pltpu.make_async_remote_copy(
            src_ref=vpiece.at[pl.ds(4 * other, 4)],
            dst_ref=vtile.at[slab],
            send_sem=t_send.at[i - 1],
            recv_sem=t_recv.at[i - 1],
            device_id={"ap": ap_of(half, other)},
            device_id_type=MESH,
        )

    for i in range(1, 4):
        tile_copy(i).start()
    vtile[slab] = vpiece[pl.ds(4 * quarter, 4)]
    for i in range(1, 4):
        tile_copy(i).wait_recv()

    lane_block = lax.broadcasted_iota(jnp.int32, (8, 128), 1) // 32

    @pl.loop(0, 4)
    def _(j):
        for a in range(8):
            tiles = [vtile[j, ky, :, 128 * a : 128 * a + 128] for ky in range(4)]
            for b in range(4):
                joined = None
                for ky in range(4):
                    shift = (32 * (ky - b)) % 128
                    moved = pltpu.roll(tiles[ky], shift, 1) if shift else tiles[ky]
                    joined = moved if joined is None else jnp.where(lane_block == ky, moved, joined)
                turn[8 * (4 * a + b) : 8 * (4 * a + b) + 8, :] = joined
        for z in range(8):
            for x in range(0, 32, 8):
                speed = turn[pl.ds(8 * x + z, 8, stride=8), :]
                coef[8 * j + z, x : x + 8, :] = speed

    source = meta[3 * shots + 16]
    source_z = source // 16384 - 32 * half
    source_x = (source // 128) % 128 - 32 * quarter
    source_in = (source_z >= 0) & (source_z < 32) & (source_x >= 0) & (source_x < 32)
    source_at = jnp.where(source_in, (source_z * 32 + source_x) * 128 + source % 128, -1)
    spot = (
        lax.broadcasted_iota(jnp.int32, (4, 8, 128), 0) * 4096
        + lax.broadcasted_iota(jnp.int32, (4, 8, 128), 1) * 128
        + lax.broadcasted_iota(jnp.int32, (4, 8, 128), 2)
    )

    def laplacian(buf, n, z, xg):
        row = 8 + 8 * xg
        column = buf[n, pl.ds(z, 12), row : row + 8, :]
        total = lap[pl.ds(z, 4), 8 * xg : 8 * xg + 8, :]
        for k in range(1, 5):
            beside = column[4 + k : 8 + k] + column[4 - k : 8 - k]
            beside = beside + (
                buf[n, pl.ds(z + 4, 4), row + k : row + k + 8, :]
                + buf[n, pl.ds(z + 4, 4), row - k : row - k + 8, :]
            )
            total = total + COEF[k] * beside
        return column[4:8], total

    def ahead(n, z, xg):
        at = (pl.ds(z, 4), slice(8 * xg, 8 * xg + 8), slice(None))
        inner = (pl.ds(z + 4, 4), slice(8 + 8 * xg, 16 + 8 * xg), slice(None))
        here, total = laplacian(fwd, n + 1, z, xg)
        fired = jnp.where(spot == source_at - (z * 4096 + xg * 1024), wav[0, n], 0.0)
        speed = coef[at]
        change = (STEP_SQUARE * speed * speed) * (total + fired)
        upd[(n,) + at] = change
        new = 2.0 * here - fwd[(n,) + inner] + change
        fwd[(n + 2,) + inner] = new
        inj[(n,) + at] = count[at] * new - inj[(n,) + at]

    def back(t, z, xg):
        n = 5 - t
        at = (pl.ds(z, 4), slice(8 * xg, 8 * xg + 8), slice(None))
        inner = (pl.ds(z + 4, 4), slice(8 + 8 * xg, 16 + 8 * xg), slice(None))
        here, total = laplacian(adj, n + 1, z, xg)
        speed = coef[at]
        new = (
            2.0 * here
            - adj[(n + 2,) + inner]
            + (STEP_SQUARE * speed * speed) * (total + inj[(n,) + at])
        )
        adj[(n,) + inner] = new
        image[at] = image[at] + new * upd[(n,) + at]

    def group_at(i):
        return 4 * (i * half + (7 - i) * (1 - half))

    def march(buf, unit, t, now, new, e):
        more = t < STEPS - 1

        @pl.loop(1, 8)
        def _(i):
            for xg in (1, 2):
                unit(t, group_at(i), xg)

        z_copy(buf, now, e).wait_recv()
        x_take(buf, now, e, chunk_at(0))
        for xg in range(4):
            unit(t, group_at(0), xg)

        @pl.when(more)
        def _():
            z_copy(buf, new, e + 1).start()

        for xg in (0, 3):
            unit(t, group_at(1), xg)

        @pl.when(more)
        def _():
            x_post(buf, new, e + 1, chunk_at(0))

        @pl.loop(1, 4)
        def _(i):
            x_take(buf, now, e, chunk_at(i))
            for g in range(2):
                for xg in (0, 3):
                    unit(t, group_at(2 * i + g), xg)

            @pl.when(more)
            def _():
                x_post(buf, new, e + 1, chunk_at(i))

        @pl.when(more)
        def _():
            lateral(buf, new)

    @pl.loop(0, STEPS)
    def _(t):
        march(fwd, ahead, t, t + 1, t + 2, t)

    lateral(adj, 6)
    image[...] = jnp.zeros(image.shape, F32)

    @pl.loop(0, STEPS)
    def _(t):
        march(adj, back, t, 6 - t, 5 - t, 6 + t)

    @pl.loop(0, 8)
    def _(g):
        at = pl.ds(4 * g, 4)
        turn[pl.ds(128 * g, 128), :] = (2.0 * image[at] / coef[at]).reshape(128, 128)

    @pl.loop(0, 4)
    def _(j):
        for a in range(8):
            rows = [turn[pl.ds(256 * j + 4 * a + b, 8, stride=32), :] for b in range(4)]
            for ky in range(4):
                joined = None
                for b in range(4):
                    shift = (32 * (b - ky)) % 128
                    moved = pltpu.roll(rows[b], shift, 1) if shift else rows[b]
                    joined = moved if joined is None else jnp.where(lane_block == b, moved, joined)
                gtile[j, ky, :, 128 * a : 128 * a + 128] = joined

    def piece_copy(i):
        other = (slab + i) % 4
        return pltpu.make_async_remote_copy(
            src_ref=gtile.at[other],
            dst_ref=gpiece.at[pl.ds(4 * quarter, 4)],
            send_sem=p_send.at[i - 1],
            recv_sem=p_recv.at[i - 1],
            device_id={"ap": 4 * half + other},
            device_id_type=MESH,
        )

    for i in range(1, 4):
        piece_copy(i).start()
    gpiece[pl.ds(4 * quarter, 4)] = gtile[slab]
    for i in range(1, 4):
        piece_copy(i).wait_recv()

    @pl.loop(0, shots)
    def _(s):
        gsend[s] = gpiece[meta[2 * shots + 16 + s]]

    grecv[me] = gpiece[meta[2 * shots + 16 + me]]
    exchange_start(gsend, grecv, g_send, g_recv)

    out[...] = jnp.zeros(out.shape, F32)

    @pl.loop(0, shots // 8)
    def _(b):
        for i in range(8):
            s = 8 * b + i

            @pl.when(s != me)
            def _():
                arrival(gsend, grecv, s, g_send, g_recv).wait_recv()

        local = [meta[shots + 8 * b + i] for i in range(8)]

        for a in range(8):
            at = (slice(None), slice(128 * a, 128 * a + 128))
            parts = [grecv[(8 * b + i,) + at] for i in range(8)]
            for tile in range(16):
                total = out[(tile,) + at]
                for i in range(8):
                    total = total + jnp.where(local[i] == tile, 1.0, 0.0) * parts[i]
                out[(tile,) + at] = total

    for f in range(4):
        for i in range(1, 4):
            field_copy(f, i).wait_send()

    @pl.loop(0, shots)
    def _(s):
        @pl.when(s != me)
        def _():
            arrival(vsend, vrecv, s, v_send, v_recv).wait_send()
            arrival(gsend, grecv, s, g_send, g_recv).wait_send()

    for i in range(1, 4):
        tile_copy(i).wait_send()
        piece_copy(i).wait_send()

    @pl.loop(0, 2 * STEPS)
    def _(e):
        z_copy(fwd, 1, e).wait_send()

        @pl.loop(0, 4)
        def _(c):
            @pl.when(has_low)
            def _():
                x_copy(e, 0, c).wait_send()

            @pl.when(has_high)
            def _():
                x_copy(e, 1, c).wait_send()


def on_device(
    velocity_tiles,
    aperture_tiles,
    source_cells,
    wavelet,
    receiver_cells,
    observed,
    field_early,
    field_late,
    adjoint_late,
    adjoint_later,
):
    shots = lax.axis_size("shot")
    me = lax.axis_index("shot")
    tiles_dev = velocity_tiles.shape[0]
    owners = aperture_tiles // tiles_dev
    matched = owners == me
    local = jnp.sum(jnp.where(matched, aperture_tiles % tiles_dev, 0), axis=1)
    local_or_none = jnp.where(jnp.any(matched, axis=1), local, -1)
    row = lax.broadcasted_iota(jnp.int32, owners.shape, 0)
    mine = jnp.sum(jnp.where(row == me, owners, 0), axis=0)
    position = jnp.sum(
        jnp.where(mine[None, :] == row, lax.broadcasted_iota(jnp.int32, owners.shape, 1), 0), axis=1
    )
    meta = jnp.concatenate([local, local_or_none, mine, position, source_cells])

    vmem = pl.BlockSpec(memory_space=pltpu.VMEM)
    smem = pl.BlockSpec(memory_space=pltpu.SMEM)
    anywhere = pl.BlockSpec(memory_space=pl.ANY)
    block = (32, 32, 128)
    dma = pltpu.SemaphoreType.DMA
    return pl.pallas_call(
        kernel,
        out_shape=jax.ShapeDtypeStruct(velocity_tiles.shape, F32),
        in_specs=[smem, smem, vmem, vmem, vmem, anywhere, anywhere, anywhere, anywhere],
        out_specs=vmem,
        scratch_shapes=[
            pltpu.VMEM((8, 40, 48, 128), F32),
            pltpu.VMEM((8, 40, 48, 128), F32),
            pltpu.VMEM((STEPS,) + block, F32),
            pltpu.VMEM((STEPS,) + block, F32),
            pltpu.VMEM(block, F32),
            pltpu.VMEM(block, F32),
            pltpu.VMEM(block, F32),
            pltpu.VMEM(block, F32),
            pltpu.VMEM((1024, 128), F32),
            pltpu.VMEM((256, 256), BF16),
            pltpu.VMEM((1024, 256), BF16),
            pltpu.VMEM((2 * STEPS, 2, 32, 4, 128), F32),
            pltpu.VMEM((2 * STEPS, 2, 32, 4, 128), F32),
            pltpu.VMEM((shots, 8, 1024), F32),
            pltpu.VMEM((shots, 8, 1024), F32),
            pltpu.VMEM((16, 8, 1024), F32),
            pltpu.VMEM((4, 4, 8, 1024), F32),
            pltpu.VMEM((4, 4, 8, 1024), F32),
            pltpu.VMEM((16, 8, 1024), F32),
            pltpu.VMEM((shots, 8, 1024), F32),
            pltpu.VMEM((shots, 8, 1024), F32),
            dma((4, 3)),
            dma((4, 3)),
            dma((4,)),
            dma((2 * STEPS,)),
            dma((2 * STEPS,)),
            dma((2 * STEPS, 2, 4)),
            dma((2 * STEPS, 2, 4)),
            dma((shots,)),
            dma((shots,)),
            dma((shots,)),
            dma((shots,)),
            dma((3,)),
            dma((3,)),
            dma((3,)),
            dma((3,)),
        ],
        compiler_params=pltpu.CompilerParams(
            collective_id=0, has_side_effects=True, vmem_limit_bytes=60 * 1024 * 1024
        ),
        name="inversion",
    )(
        meta,
        wavelet,
        receiver_cells,
        observed,
        velocity_tiles,
        field_early,
        field_late,
        adjoint_late,
        adjoint_later,
    )


def solution(mesh):
    placed = (
        P("shot", "ap", None),
        P(),
        P("shot"),
        P("shot", None),
        P("shot", None),
        P("shot", None, None),
        P("shot", "ap", None, None),
        P("shot", "ap", None, None),
        P("shot", "ap", None, None),
        P("shot", "ap", None, None),
    )
    return jax.shard_map(
        on_device, mesh=mesh, in_specs=placed, out_specs=P("shot", "ap", None), check_vma=False
    )
```

```python
import functools

import jax
import jax.numpy as jnp
from jax import lax
from jax.experimental import pallas as pl
from jax.experimental.pallas import tpu as pltpu
from jax.sharding import PartitionSpec as P

COEF = (-205.0 / 72.0, 8.0 / 5.0, -1.0 / 5.0, 8.0 / 315.0, -1.0 / 560.0)
STEP_SQUARE = 0.01
MESH = pl.DeviceIdType.MESH
STEPS = 6
F32 = jnp.float32
BF16 = jnp.bfloat16
FACE_ORDER = (1, 2, 0, 3)
Z_ORDER = (4, 3, 5, 2, 6, 1, 7, 0)


def ap_of(half, quarter):
    mirror = quarter // 2
    y = ((quarter + 1) // 2) % 2
    x = mirror + half * (1 - 2 * mirror)
    return 4 * half + 2 * x + y


def split(value):
    high = value.astype(BF16)
    return high, (value - high.astype(F32)).astype(BF16)


def kernel(
    tile_sent, tile_kept, tile_owner, tile_place, source_cell, wav, cells, observed, vel, early, late, a_late, a_later, out,
    fwd, adj, upd, inj, coef, count, image, lap, turn, ymat, hot,
    xs, xr, vsend, vrecv0, vrecv1, vpiece, vtile0, vtile1, gtile, gpiece0, gpiece1,
    gsend, grecv0, grecv1,
    f_send, f_recv, f_loc, z_send, z_recv, x_send, x_recv,
    v_send, v_recv, g_send, g_recv, t_send, t_recv, p_send, p_recv,
):
    vrecv, vtile, gpiece, grecv = (
        (vrecv0, vrecv1), (vtile0, vtile1), (gpiece0, gpiece1), (grecv0, grecv1)
    )
    shots = lax.axis_size("shot")
    me = lax.axis_index("shot")
    ap = lax.axis_index("ap")
    half = ap // 4
    slab = ap % 4
    xl = slab // 2
    yl = slab % 2
    mirror = xl + half * (1 - 2 * xl)
    quarter = yl + mirror * (3 - 2 * yl)
    has_low = quarter > 0
    has_high = quarter < 3

    fields = ((late, fwd, 1), (early, fwd, 0), (a_late, adj, 6), (a_later, adj, 7))

    def own_copy(f):
        source, buf, n = fields[f]
        return pltpu.make_async_copy(
            source.at[0, :, pl.ds(32 * quarter, 32), :],
            buf.at[n, pl.ds(4 + 8 * slab, 8), pl.ds(8, 32), :],
            f_loc.at[f],
        )

    def field_copy(f, i):
        source, buf, n = fields[f]
        other = (quarter + i) % 4
        return pltpu.make_async_remote_copy(
            src_ref=source.at[0, :, pl.ds(32 * other, 32), :],
            dst_ref=buf.at[n, pl.ds(4 + 8 * slab, 8), pl.ds(8, 32), :],
            send_sem=f_send.at[f, i - 1],
            recv_sem=f_recv.at[f, i - 1],
            device_id={"ap": ap_of(half, other)},
            device_id_type=MESH,
        )

    barrier = pltpu.get_barrier_semaphore()

    side = (me // 2) % 2
    beside = ap + 1 - 2 * (ap % 2)

    def crossed(shot):
        return (shot // 2 + side) % 2

    @pl.loop(1, shots)
    def _(d):
        other = (me + d) % shots
        pl.semaphore_signal(
            barrier,
            inc=1,
            device_id={"shot": other, "ap": ap + (beside - ap) * crossed(other)},
            device_id_type=MESH,
        )

    for i in range(1, 4):
        pl.semaphore_signal(
            barrier, inc=1, device_id={"ap": ap_of(half, (quarter + i) % 4)}, device_id_type=MESH
        )
    partner = ap_of(1 - half, quarter)
    pl.semaphore_signal(barrier, inc=1, device_id={"ap": partner}, device_id_type=MESH)

    for f in range(4):
        own_copy(f).start()

    @pl.loop(0, shots)
    def _(s):
        vsend[s] = vel[tile_sent[s]]

    for h in range(2):
        vrecv[h][me] = vel[tile_sent[me], :, 512 * h : 512 * h + 512]

    pl.semaphore_wait(barrier, shots - 1 + 4)

    for f in (0, 1):
        for i in range(1, 4):
            field_copy(f, i).start()

    def part(h):
        return pl.ds(512 * h, 512)

    def exchange_copy(src, dst, target, cross, h, send, recv):
        return pltpu.make_async_remote_copy(
            src_ref=src.at[target, :, part(h)],
            dst_ref=dst[h].at[me],
            send_sem=send.at[target, h],
            recv_sem=recv.at[me, h],
            device_id={"shot": target, "ap": beside if cross else ap},
            device_id_type=MESH,
        )

    def arrival(src, dst, origin, h, send, recv):
        return pltpu.make_async_remote_copy(
            src_ref=src.at[origin, :, part(h)],
            dst_ref=dst[h].at[origin],
            send_sem=send.at[origin, h],
            recv_sem=recv.at[origin, h],
            device_id={"shot": origin},
            device_id_type=MESH,
        )

    def exchange_start(src, dst, core, h, send, recv):
        planes = shots // 4
        for dz in range(planes):
            for dy in range(2):
                step = Z_ORDER[dz] if planes == 8 else dz
                target = ((me // 4 + step) % planes) * 4 + ((me // 2 + dy) % 2) * 2 + core

                @pl.when(target != me)
                def _():
                    exchange_copy(src, dst, target, dy, h, send, recv).start()

    for h in range(2):
        for core in range(2):
            exchange_start(vsend, vrecv, core, h, v_send, v_recv)

    for f in (2, 3):
        for i in range(1, 4):
            field_copy(f, i).start()

    distance = jnp.abs(
        lax.broadcasted_iota(jnp.int32, (128, 128), 0)
        - lax.broadcasted_iota(jnp.int32, (128, 128), 1)
    )
    band = jnp.where(distance == 0, 3.0 * COEF[0], 0.0)
    for k in range(1, 5):
        band = jnp.where(distance == k, COEF[k], band)
    band_high, band_low = split(band)
    ymat[0:128, 0:128] = band_high
    ymat[128:256, 0:128] = band_high
    ymat[0:128, 128:256] = band_low
    ymat[128:256, 128:256] = jnp.zeros((128, 128), BF16)

    @pl.loop(1, 7)
    def _(n):
        for buf in (fwd, adj):
            buf[n, pl.ds(36 * half, 4), 8:40, :] = jnp.zeros((4, 32, 128), F32)

        @pl.loop(0, 8)
        def _(g):
            for buf in (fwd, adj):
                buf[n, pl.ds(4 + 4 * g, 4), 0:8, :] = jnp.zeros((4, 8, 128), F32)
                buf[n, pl.ds(4 + 4 * g, 4), 40:48, :] = jnp.zeros((4, 8, 128), F32)

    flat = cells[0:1, :]
    z_at = flat // 16384 - 32 * half
    x_at = (flat // 128) % 128 - 32 * quarter
    y_at = flat % 128
    inside = (z_at >= 0) & (z_at < 32) & (x_at >= 0) & (x_at < 32)
    row_at = jnp.where(inside, z_at * 32 + x_at, -1)
    nrec = cells.shape[1]

    @pl.loop(0, 16)
    def _(b):
        rows = lax.broadcasted_iota(jnp.int32, (64, nrec), 0) + b * 64
        hot[pl.ds(b * 64, 64), :] = jnp.where(rows == row_at, 1.0, 0.0).astype(BF16)

    lanes = jnp.where(
        lax.broadcasted_iota(jnp.int32, (128, nrec), 0) == y_at, 1.0, 0.0
    )
    contract = (((1,), (1,)), ((), ()))
    lanes_low = lanes.astype(BF16)

    @pl.loop(0, 4)
    def _(b):
        found = lax.dot_general(
            hot[pl.ds(b * 256, 256), :], lanes_low, contract, preferred_element_type=F32
        )
        count[pl.ds(8 * b, 8), :, :] = found.reshape(8, 32, 128)

    for n in range(STEPS):
        high, low = split(lanes * observed[0, n : n + 1, :])
        both = jnp.concatenate([high, low], axis=0)

        @pl.loop(0, 4)
        def _(b):
            found = lax.dot_general(
                hot[pl.ds(b * 256, 256), :], both, contract, preferred_element_type=F32
            )
            inj[n, pl.ds(8 * b, 8), :, :] = (found[:, 0:128] + found[:, 128:256]).reshape(
                8, 32, 128
            )

    def z_copy(buf, n, e, xg):
        return pltpu.make_async_remote_copy(
            src_ref=buf.at[n, pl.ds(32 - 28 * half, 4), pl.ds(8 + 8 * xg, 8), :],
            dst_ref=buf.at[n, pl.ds(36 * half, 4), pl.ds(8 + 8 * xg, 8), :],
            send_sem=z_send.at[e, xg],
            recv_sem=z_recv.at[e, xg],
            device_id={"ap": partner},
            device_id_type=MESH,
        )

    def x_copy(e, side, c):
        other = ap_of(half, quarter + (2 * side - 1))
        return pltpu.make_async_remote_copy(
            src_ref=xs.at[e, side, pl.ds(8 * c, 8)],
            dst_ref=xr.at[e, 1 - side, pl.ds(8 * c, 8)],
            send_sem=x_send.at[e, side, c],
            recv_sem=x_recv.at[e, 1 - side, c],
            device_id={"ap": other},
            device_id_type=MESH,
        )

    def x_arrival(e, side, c):
        other = ap_of(half, quarter + (2 * side - 1))
        return pltpu.make_async_remote_copy(
            src_ref=xs.at[e, side, pl.ds(8 * c, 8)],
            dst_ref=xr.at[e, side, pl.ds(8 * c, 8)],
            send_sem=x_send.at[e, side, c],
            recv_sem=x_recv.at[e, side, c],
            device_id={"ap": other},
            device_id_type=MESH,
        )

    def x_post(buf, n, e, c):
        at = pl.ds(4 + 8 * c, 8)

        @pl.when(has_low)
        def _():
            xs[e, 0, pl.ds(8 * c, 8)] = buf[n, at, 8:12, :]
            x_copy(e, 0, c).start()

        @pl.when(has_high)
        def _():
            xs[e, 1, pl.ds(8 * c, 8)] = buf[n, at, 36:40, :]
            x_copy(e, 1, c).start()

    def x_take(buf, n, e, c):
        at = pl.ds(4 + 8 * c, 8)

        @pl.when(has_low)
        def _():
            x_arrival(e, 0, c).wait_recv()
            buf[n, at, 4:8, :] = xr[e, 0, pl.ds(8 * c, 8)]

        @pl.when(has_high)
        def _():
            x_arrival(e, 1, c).wait_recv()
            buf[n, at, 40:44, :] = xr[e, 1, pl.ds(8 * c, 8)]

    def chunk_at(i):
        return i * half + (3 - i) * (1 - half)

    def fields_ready(f):
        own_copy(f).wait()
        for i in range(1, 4):
            field_copy(f, i).wait_recv()

    def lateral(buf, n):
        @pl.loop(0, 4)
        def _(c):
            here = buf[n, pl.ds(4 + 8 * c, 8), 8:40, :].reshape(256, 128)
            both = jnp.concatenate(split(here), axis=1)
            found = jnp.dot(both, ymat[...], preferred_element_type=F32)
            lap[pl.ds(8 * c, 8), :, :] = (found[:, 0:128] + found[:, 128:256]).reshape(8, 32, 128)

    def first_post(f, e):
        buf, n = fields[f][1:]
        fields_ready(f)
        for xg in FACE_ORDER:
            z_copy(buf, n, e, xg).start()
        for i in range(4):
            x_post(buf, n, e, chunk_at(i))

    first_post(0, 0)
    fields_ready(1)
    lateral(fwd, 1)

    def tile_copy(i, h):
        other = (quarter + i) % 4
        return pltpu.make_async_remote_copy(
            src_ref=vpiece.at[pl.ds(4 * other, 4), :, part(h)],
            dst_ref=vtile[h].at[slab],
            send_sem=t_send.at[i - 1, h],
            recv_sem=t_recv.at[i - 1, h],
            device_id={"ap": ap_of(half, other)},
            device_id_type=MESH,
        )

    turned = [crossed(tile_owner[4 * quarter + ky]) for ky in range(4)]
    def at_slab(j, ky):
        return j + turned[ky] * (1 - 2 * (j % 2))

    lane_block = lax.broadcasted_iota(jnp.int32, (8, 128), 1) // 32

    for h in range(2):
        lanes_h = slice(512 * h, 512 * h + 512)

        @pl.loop(0, shots)
        def _(s):
            @pl.when(s != me)
            def _():
                arrival(vsend, vrecv, s, h, v_send, v_recv).wait_recv()

        @pl.loop(0, 16)
        def _(k):
            vpiece[k, :, lanes_h] = vrecv[h][tile_owner[k]]

        for i in range(1, 4):
            tile_copy(i, h).start()
        vtile[h][slab] = vpiece[pl.ds(4 * quarter, 4), :, lanes_h]

    for h in range(2):
        for i in range(1, 4):
            tile_copy(i, h).wait_recv()

        @pl.loop(0, 4)
        def _(j):
            for a in range(4 * h, 4 * h + 4):
                tiles = [
                    vtile[h][at_slab(j, ky), ky, :, 128 * (a % 4) : 128 * (a % 4) + 128]
                    for ky in range(4)
                ]
                for b in range(4):
                    joined = None
                    for ky in range(4):
                        shift = (32 * (ky - b)) % 128
                        moved = pltpu.roll(tiles[ky], shift, 1) if shift else tiles[ky]
                        joined = (
                            moved if joined is None else jnp.where(lane_block == ky, moved, joined)
                        )
                    turn[8 * (4 * a + b) : 8 * (4 * a + b) + 8, :] = joined
            for z in range(8):
                for x in (16 * h, 16 * h + 8):
                    coef[8 * j + z, x : x + 8, :] = turn[pl.ds(8 * x + z, 8, stride=8), :]

    source = source_cell[0]
    source_z = source // 16384 - 32 * half
    source_x = (source // 128) % 128 - 32 * quarter
    source_in = (source_z >= 0) & (source_z < 32) & (source_x >= 0) & (source_x < 32)
    source_at = jnp.where(source_in, (source_z * 32 + source_x) * 128 + source % 128, -1)
    spot = (
        lax.broadcasted_iota(jnp.int32, (4, 8, 128), 0) * 4096
        + lax.broadcasted_iota(jnp.int32, (4, 8, 128), 1) * 128
        + lax.broadcasted_iota(jnp.int32, (4, 8, 128), 2)
    )

    def laplacian(buf, n, z, xg):
        row = 8 + 8 * xg
        column = buf[n, pl.ds(z, 12), row : row + 8, :]
        total = lap[pl.ds(z, 4), 8 * xg : 8 * xg + 8, :]
        for k in range(1, 5):
            beside = column[4 + k : 8 + k] + column[4 - k : 8 - k]
            beside = beside + (
                buf[n, pl.ds(z + 4, 4), row + k : row + k + 8, :]
                + buf[n, pl.ds(z + 4, 4), row - k : row - k + 8, :]
            )
            total = total + COEF[k] * beside
        return column[4:8], total

    def ahead(n, z, xg):
        at = (pl.ds(z, 4), slice(8 * xg, 8 * xg + 8), slice(None))
        inner = (pl.ds(z + 4, 4), slice(8 + 8 * xg, 16 + 8 * xg), slice(None))
        here, total = laplacian(fwd, n + 1, z, xg)
        fired = jnp.where(spot == source_at - (z * 4096 + xg * 1024), wav[0, n], 0.0)
        speed = coef[at]
        change = (STEP_SQUARE * speed * speed) * (total + fired)
        upd[(n,) + at] = change
        new = 2.0 * here - fwd[(n,) + inner] + change
        fwd[(n + 2,) + inner] = new
        inj[(n,) + at] = count[at] * new - inj[(n,) + at]

    def back(t, z, xg):
        n = 5 - t
        at = (pl.ds(z, 4), slice(8 * xg, 8 * xg + 8), slice(None))
        inner = (pl.ds(z + 4, 4), slice(8 + 8 * xg, 16 + 8 * xg), slice(None))
        here, total = laplacian(adj, n + 1, z, xg)
        speed = coef[at]
        new = (
            2.0 * here
            - adj[(n + 2,) + inner]
            + (STEP_SQUARE * speed * speed) * (total + inj[(n,) + at])
        )
        adj[(n,) + inner] = new
        image[at] = image[at] + new * upd[(n,) + at]

    def group_at(i):
        return 4 * (i * half + (7 - i) * (1 - half))

    def march(buf, unit, t, now, new, e):
        more = t < STEPS - 1

        @pl.loop(1, 8)
        def _(i):
            for xg in (1, 2):
                unit(t, group_at(i), xg)

        for xg in FACE_ORDER:
            if xg == 0:
                x_take(buf, now, e, chunk_at(0))
            z_copy(buf, now, e, xg).wait_recv()
            unit(t, group_at(0), xg)

            @pl.when(more)
            def _():
                z_copy(buf, new, e + 1, xg).start()

        for xg in (0, 3):
            unit(t, group_at(1), xg)

        @pl.when(more)
        def _():
            x_post(buf, new, e + 1, chunk_at(0))

        @pl.loop(1, 4)
        def _(i):
            x_take(buf, now, e, chunk_at(i))
            for g in range(2):
                for xg in (0, 3):
                    unit(t, group_at(2 * i + g), xg)

            @pl.when(more)
            def _():
                x_post(buf, new, e + 1, chunk_at(i))

        @pl.when(more)
        def _():
            lateral(buf, new)

    @pl.loop(0, STEPS)
    def _(t):
        march(fwd, ahead, t, t + 1, t + 2, t)

        @pl.when(t == 3)
        def _():
            first_post(2, 6)

    fields_ready(3)
    lateral(adj, 6)
    image[...] = jnp.zeros(image.shape, F32)

    @pl.loop(0, STEPS)
    def _(t):
        march(adj, back, t, 6 - t, 5 - t, 6 + t)

    @pl.loop(0, 8)
    def _(g):
        at = pl.ds(4 * g, 4)
        turn[pl.ds(128 * g, 128), :] = (image[at] / coef[at]).reshape(128, 128)

    def piece_copy(i, h):
        other = (slab + i) % 4
        return pltpu.make_async_remote_copy(
            src_ref=gtile.at[other, :, :, part(h)],
            dst_ref=gpiece[h].at[pl.ds(4 * quarter, 4)],
            send_sem=p_send.at[i - 1, h],
            recv_sem=p_recv.at[i - 1, h],
            device_id={"ap": 4 * half + other},
            device_id_type=MESH,
        )

    for h in range(2):
        lanes_h = slice(512 * h, 512 * h + 512)

        @pl.loop(0, 4)
        def _(j):
            for a in range(4 * h, 4 * h + 4):
                for ky in range(4):
                    base = 256 * at_slab(j, ky) + 4 * a
                    rows = [turn[pl.ds(base + b, 8, stride=32), :] for b in range(4)]
                    joined = None
                    for b in range(4):
                        shift = (32 * (b - ky)) % 128
                        moved = pltpu.roll(rows[b], shift, 1) if shift else rows[b]
                        joined = (
                            moved if joined is None else jnp.where(lane_block == b, moved, joined)
                        )
                    gtile[j, ky, :, 128 * a : 128 * a + 128] = joined

        for i in range(1, 4):
            piece_copy(i, h).start()
        gpiece[h][pl.ds(4 * quarter, 4)] = gtile[slab, :, :, lanes_h]

    for h in range(2):
        lanes_h = slice(512 * h, 512 * h + 512)
        for i in range(1, 4):
            piece_copy(i, h).wait_recv()

        @pl.loop(0, shots)
        def _(s):
            gsend[s, :, lanes_h] = gpiece[h][tile_place[s]]

        grecv[h][me] = gpiece[h][tile_place[me]]
        for core in range(2):
            exchange_start(gsend, grecv, core, h, g_send, g_recv)

    out[...] = jnp.zeros(out.shape, F32)

    for h in range(2):

        @pl.loop(0, shots // 8)
        def _(b):
            for i in range(8):
                s = 8 * b + i

                @pl.when(s != me)
                def _():
                    arrival(gsend, grecv, s, h, g_send, g_recv).wait_recv()

            local = [tile_kept[8 * b + i] for i in range(8)]

            for a in range(4 * h, 4 * h + 4):
                at = (slice(None), slice(128 * a, 128 * a + 128))
                here = (slice(None), slice(128 * (a % 4), 128 * (a % 4) + 128))
                parts = [grecv[h][(8 * b + i,) + here] for i in range(8)]
                for tile in range(16):
                    total = out[(tile,) + at]
                    for i in range(8):
                        total = total + jnp.where(local[i] == tile, 1.0, 0.0) * parts[i]
                    out[(tile,) + at] = total

    for f in range(4):
        for i in range(1, 4):
            field_copy(f, i).wait_send()

    @pl.loop(0, shots)
    def _(s):
        @pl.when(s != me)
        def _():
            for h in range(2):
                arrival(vsend, vrecv, s, h, v_send, v_recv).wait_send()
                arrival(gsend, grecv, s, h, g_send, g_recv).wait_send()

    for h in range(2):
        for i in range(1, 4):
            tile_copy(i, h).wait_send()
            piece_copy(i, h).wait_send()

    @pl.loop(0, 2 * STEPS)
    def _(e):
        for xg in range(4):
            z_copy(fwd, 1, e, xg).wait_send()

        @pl.loop(0, 4)
        def _(c):
            @pl.when(has_low)
            def _():
                x_copy(e, 0, c).wait_send()

            @pl.when(has_high)
            def _():
                x_copy(e, 1, c).wait_send()


def on_device(
    velocity_tiles,
    aperture_tiles,
    source_cells,
    wavelet,
    receiver_cells,
    observed,
    field_early,
    field_late,
    adjoint_late,
    adjoint_later,
):
    shots = lax.axis_size("shot")
    me = lax.axis_index("shot")
    tiles_dev = velocity_tiles.shape[0]
    owners = aperture_tiles // tiles_dev
    matched = owners == me
    local = jnp.sum(jnp.where(matched, aperture_tiles % tiles_dev, 0), axis=1)
    local_or_none = jnp.where(jnp.any(matched, axis=1), local, -1)
    row = lax.broadcasted_iota(jnp.int32, owners.shape, 0)
    mine = jnp.sum(jnp.where(row == me, owners, 0), axis=0)
    position = jnp.sum(
        jnp.where(mine[None, :] == row, lax.broadcasted_iota(jnp.int32, owners.shape, 1), 0), axis=1
    )

    vmem = pl.BlockSpec(memory_space=pltpu.VMEM)
    smem = pl.BlockSpec(memory_space=pltpu.SMEM)
    anywhere = pl.BlockSpec(memory_space=pl.ANY)
    block = (32, 32, 128)
    dma = pltpu.SemaphoreType.DMA
    half_gradient = pl.pallas_call(
        kernel,
        out_shape=jax.ShapeDtypeStruct(velocity_tiles.shape, F32),
        in_specs=[smem] * 6 + [vmem, vmem, vmem, anywhere, anywhere, anywhere, anywhere],
        out_specs=vmem,
        scratch_shapes=[
            pltpu.VMEM((8, 40, 48, 128), F32),
            pltpu.VMEM((8, 40, 48, 128), F32),
            pltpu.VMEM((STEPS,) + block, F32),
            pltpu.VMEM((STEPS,) + block, F32),
            pltpu.VMEM(block, F32),
            pltpu.VMEM(block, F32),
            pltpu.VMEM(block, F32),
            pltpu.VMEM(block, F32),
            pltpu.VMEM((1024, 128), F32),
            pltpu.VMEM((256, 256), BF16),
            pltpu.VMEM((1024, 256), BF16),
            pltpu.VMEM((2 * STEPS, 2, 32, 4, 128), F32),
            pltpu.VMEM((2 * STEPS, 2, 32, 4, 128), F32),
            pltpu.VMEM((shots, 8, 1024), F32),
            pltpu.VMEM((shots, 8, 512), F32),
            pltpu.VMEM((shots, 8, 512), F32),
            pltpu.VMEM((16, 8, 1024), F32),
            pltpu.VMEM((4, 4, 8, 512), F32),
            pltpu.VMEM((4, 4, 8, 512), F32),
            pltpu.VMEM((4, 4, 8, 1024), F32),
            pltpu.VMEM((16, 8, 512), F32),
            pltpu.VMEM((16, 8, 512), F32),
            pltpu.VMEM((shots, 8, 1024), F32),
            pltpu.VMEM((shots, 8, 512), F32),
            pltpu.VMEM((shots, 8, 512), F32),
            dma((4, 3)),
            dma((4, 3)),
            dma((4,)),
            dma((2 * STEPS, 4)),
            dma((2 * STEPS, 4)),
            dma((2 * STEPS, 2, 4)),
            dma((2 * STEPS, 2, 4)),
            dma((shots, 2)),
            dma((shots, 2)),
            dma((shots, 2)),
            dma((shots, 2)),
            dma((3, 2)),
            dma((3, 2)),
            dma((3, 2)),
            dma((3, 2)),
        ],
        compiler_params=pltpu.CompilerParams(
            collective_id=0, has_side_effects=True, vmem_limit_bytes=60 * 1024 * 1024
        ),
        name="inversion",
    )(
        local,
        local_or_none,
        mine,
        position,
        source_cells,
        wavelet,
        receiver_cells,
        observed,
        velocity_tiles,
        field_early,
        field_late,
        adjoint_late,
        adjoint_later,
    )
    return 2.0 * half_gradient


def solution(mesh):
    placed = (
        P("shot", "ap", None),
        P(),
        P("shot"),
        P("shot", None),
        P("shot", None),
        P("shot", None, None),
        P("shot", "ap", None, None),
        P("shot", "ap", None, None),
        P("shot", "ap", None, None),
        P("shot", "ap", None, None),
    )
    return jax.shard_map(
        on_device, mesh=mesh, in_specs=placed, out_specs=P("shot", "ap", None), check_vma=False
    )
```

```python
import functools

import jax
import jax.numpy as jnp
from jax import lax
from jax.experimental import pallas as pl
from jax.experimental.pallas import tpu as pltpu
from jax.sharding import PartitionSpec as P

COEF = (-205.0 / 72.0, 8.0 / 5.0, -1.0 / 5.0, 8.0 / 315.0, -1.0 / 560.0)
STEP_SQUARE = 0.01
MESH = pl.DeviceIdType.MESH
STEPS = 6
F32 = jnp.float32
BF16 = jnp.bfloat16
PARTS = 2
BLOCKS = 8 // PARTS
WIDE = 128 * BLOCKS
FACE_ORDER = (1, 2, 0, 3)
Z_ORDER = (4, 3, 5, 2, 6, 1, 7, 0)


def ap_of(half, quarter):
    mirror = quarter // 2
    y = ((quarter + 1) // 2) % 2
    x = mirror + half * (1 - 2 * mirror)
    return 4 * half + 2 * x + y


def split(value):
    high = value.astype(BF16)
    return high, (value - high.astype(F32)).astype(BF16)


def kernel(
    table, wav, cells, observed_at, vel_at, early, late, a_late, a_later, out,
    fwd, adj, upd, inj, coef, count, image, lap, turn, ymat, hot,
    xs, xr, vsend, vrecv, vpiece, vtile, gtile, gpiece, gsend, grecv, vel, observed,
    i_sem, f_send, f_recv, f_loc, z_send, z_recv, x_send, x_recv,
    v_send, v_recv, g_send, g_recv, t_send, t_recv, p_send, p_recv,
):
    shots = lax.axis_size("shot")
    me = lax.axis_index("shot")
    ap = lax.axis_index("ap")
    half = ap // 4
    slab = ap % 4
    xl = slab // 2
    yl = slab % 2
    mirror = xl + half * (1 - 2 * xl)
    quarter = yl + mirror * (3 - 2 * yl)
    has_low = quarter > 0
    has_high = quarter < 3

    fields = ((late, fwd, 1), (early, fwd, 0), (a_late, adj, 6), (a_later, adj, 7))

    def own_copy(f):
        source, buf, n = fields[f]
        return pltpu.make_async_copy(
            source.at[0, :, pl.ds(32 * quarter, 32), :],
            buf.at[n, pl.ds(4 + 8 * slab, 8), pl.ds(8, 32), :],
            f_loc.at[f],
        )

    def field_copy(f, i):
        source, buf, n = fields[f]
        other = (quarter + i) % 4
        return pltpu.make_async_remote_copy(
            src_ref=source.at[0, :, pl.ds(32 * other, 32), :],
            dst_ref=buf.at[n, pl.ds(4 + 8 * slab, 8), pl.ds(8, 32), :],
            send_sem=f_send.at[f, i - 1],
            recv_sem=f_recv.at[f, i - 1],
            device_id={"ap": ap_of(half, other)},
            device_id_type=MESH,
        )

    vel_copy = pltpu.make_async_copy(vel_at, vel, i_sem.at[0])
    observed_copy = pltpu.make_async_copy(observed_at.at[0], observed, i_sem.at[1])
    vel_copy.start()
    barrier = pltpu.get_barrier_semaphore()

    side = (me // 2) % 2
    beside = ap + 1 - 2 * (ap % 2)

    def crossed(shot):
        return (shot // 2 + side) % 2

    @pl.loop(1, shots)
    def _(d):
        other = (me + d) % shots
        pl.semaphore_signal(
            barrier,
            inc=1,
            device_id={"shot": other, "ap": ap + (beside - ap) * crossed(other)},
            device_id_type=MESH,
        )

    for i in range(1, 4):
        pl.semaphore_signal(
            barrier, inc=1, device_id={"ap": ap_of(half, (quarter + i) % 4)}, device_id_type=MESH
        )
    partner = ap_of(1 - half, quarter)
    pl.semaphore_signal(barrier, inc=1, device_id={"ap": partner}, device_id_type=MESH)

    for f in range(4):
        own_copy(f).start()
    observed_copy.start()
    vel_copy.wait()

    @pl.loop(0, shots)
    def _(s):
        vsend[s] = vel[table[s]]

    for h in range(PARTS):
        vrecv[h][me] = vel[table[me], :, WIDE * h : WIDE * h + WIDE]

    pl.semaphore_wait(barrier, shots - 1 + 4)

    for f in (0, 1):
        for i in range(1, 4):
            field_copy(f, i).start()

    def part(h):
        return pl.ds(WIDE * h, WIDE)

    def exchange_copy(src, dst, target, cross, h, send, recv):
        return pltpu.make_async_remote_copy(
            src_ref=src.at[target, :, part(h)],
            dst_ref=dst[h].at[me],
            send_sem=send.at[target, h],
            recv_sem=recv.at[me, h],
            device_id={"shot": target, "ap": beside if cross else ap},
            device_id_type=MESH,
        )

    def arrival(src, dst, origin, h, send, recv):
        return pltpu.make_async_remote_copy(
            src_ref=src.at[origin, :, part(h)],
            dst_ref=dst[h].at[origin],
            send_sem=send.at[origin, h],
            recv_sem=recv.at[origin, h],
            device_id={"shot": origin},
            device_id_type=MESH,
        )

    def exchange_start(src, dst, core, h, send, recv):
        planes = shots // 4
        for dz in range(planes):
            for dy in range(2):
                step = Z_ORDER[dz] if planes == 8 else dz
                target = ((me // 4 + step) % planes) * 4 + ((me // 2 + dy) % 2) * 2 + core

                @pl.when(target != me)
                def _():
                    exchange_copy(src, dst, target, dy, h, send, recv).start()

    for h in range(PARTS):
        for core in range(2):
            exchange_start(vsend, vrecv, core, h, v_send, v_recv)

    for f in (2, 3):
        for i in range(1, 4):
            field_copy(f, i).start()

    distance = jnp.abs(
        lax.broadcasted_iota(jnp.int32, (128, 128), 0)
        - lax.broadcasted_iota(jnp.int32, (128, 128), 1)
    )
    band = jnp.where(distance == 0, 3.0 * COEF[0], 0.0)
    for k in range(1, 5):
        band = jnp.where(distance == k, COEF[k], band)
    band_high, band_low = split(band)
    ymat[0:128, 0:128] = band_high
    ymat[128:256, 0:128] = band_high
    ymat[0:128, 128:256] = band_low
    ymat[128:256, 128:256] = jnp.zeros((128, 128), BF16)

    @pl.loop(1, 7)
    def _(n):
        for buf in (fwd, adj):
            buf[n, pl.ds(36 * half, 4), 8:40, :] = jnp.zeros((4, 32, 128), F32)

        @pl.loop(0, 8)
        def _(g):
            for buf in (fwd, adj):
                buf[n, pl.ds(4 + 4 * g, 4), 0:8, :] = jnp.zeros((4, 8, 128), F32)
                buf[n, pl.ds(4 + 4 * g, 4), 40:48, :] = jnp.zeros((4, 8, 128), F32)

    flat = cells[0:1, :]
    z_at = flat // 16384 - 32 * half
    x_at = (flat // 128) % 128 - 32 * quarter
    y_at = flat % 128
    inside = (z_at >= 0) & (z_at < 32) & (x_at >= 0) & (x_at < 32)
    row_at = jnp.where(inside, z_at * 32 + x_at, -1)
    nrec = cells.shape[1]

    @pl.loop(0, 16)
    def _(b):
        rows = lax.broadcasted_iota(jnp.int32, (64, nrec), 0) + b * 64
        hot[pl.ds(b * 64, 64), :] = jnp.where(rows == row_at, 1.0, 0.0).astype(BF16)

    lanes = jnp.where(
        lax.broadcasted_iota(jnp.int32, (128, nrec), 0) == y_at, 1.0, 0.0
    )
    contract = (((1,), (1,)), ((), ()))
    lanes_low = lanes.astype(BF16)

    @pl.loop(0, 4)
    def _(b):
        found = lax.dot_general(
            hot[pl.ds(b * 256, 256), :], lanes_low, contract, preferred_element_type=F32
        )
        count[pl.ds(8 * b, 8), :, :] = found.reshape(8, 32, 128)

    observed_copy.wait()
    for n in range(STEPS):
        high, low = split(lanes * observed[n : n + 1, :])
        both = jnp.concatenate([high, low], axis=0)

        @pl.loop(0, 4)
        def _(b):
            found = lax.dot_general(
                hot[pl.ds(b * 256, 256), :], both, contract, preferred_element_type=F32
            )
            inj[n, pl.ds(8 * b, 8), :, :] = (found[:, 0:128] + found[:, 128:256]).reshape(
                8, 32, 128
            )

    def z_copy(buf, n, e, xg):
        return pltpu.make_async_remote_copy(
            src_ref=buf.at[n, pl.ds(32 - 28 * half, 4), pl.ds(8 + 8 * xg, 8), :],
            dst_ref=buf.at[n, pl.ds(36 * half, 4), pl.ds(8 + 8 * xg, 8), :],
            send_sem=z_send.at[e, xg],
            recv_sem=z_recv.at[e, xg],
            device_id={"ap": partner},
            device_id_type=MESH,
        )

    def x_copy(e, side, c):
        other = ap_of(half, quarter + (2 * side - 1))
        return pltpu.make_async_remote_copy(
            src_ref=xs.at[e, side, pl.ds(8 * c, 8)],
            dst_ref=xr.at[e, 1 - side, pl.ds(8 * c, 8)],
            send_sem=x_send.at[e, side, c],
            recv_sem=x_recv.at[e, 1 - side, c],
            device_id={"ap": other},
            device_id_type=MESH,
        )

    def x_arrival(e, side, c):
        other = ap_of(half, quarter + (2 * side - 1))
        return pltpu.make_async_remote_copy(
            src_ref=xs.at[e, side, pl.ds(8 * c, 8)],
            dst_ref=xr.at[e, side, pl.ds(8 * c, 8)],
            send_sem=x_send.at[e, side, c],
            recv_sem=x_recv.at[e, side, c],
            device_id={"ap": other},
            device_id_type=MESH,
        )

    def x_post(buf, n, e, c):
        at = pl.ds(4 + 8 * c, 8)

        @pl.when(has_low)
        def _():
            xs[e, 0, pl.ds(8 * c, 8)] = buf[n, at, 8:12, :]
            x_copy(e, 0, c).start()

        @pl.when(has_high)
        def _():
            xs[e, 1, pl.ds(8 * c, 8)] = buf[n, at, 36:40, :]
            x_copy(e, 1, c).start()

    def x_take(buf, n, e, c):
        at = pl.ds(4 + 8 * c, 8)

        @pl.when(has_low)
        def _():
            x_arrival(e, 0, c).wait_recv()
            buf[n, at, 4:8, :] = xr[e, 0, pl.ds(8 * c, 8)]

        @pl.when(has_high)
        def _():
            x_arrival(e, 1, c).wait_recv()
            buf[n, at, 40:44, :] = xr[e, 1, pl.ds(8 * c, 8)]

    def chunk_at(i):
        return i * half + (3 - i) * (1 - half)

    def fields_ready(f):
        own_copy(f).wait()
        for i in range(1, 4):
            field_copy(f, i).wait_recv()

    def lateral(buf, n):
        @pl.loop(0, 4)
        def _(c):
            here = buf[n, pl.ds(4 + 8 * c, 8), 8:40, :].reshape(256, 128)
            both = jnp.concatenate(split(here), axis=1)
            found = jnp.dot(both, ymat[...], preferred_element_type=F32)
            lap[pl.ds(8 * c, 8), :, :] = (found[:, 0:128] + found[:, 128:256]).reshape(8, 32, 128)

    def first_post(f, e):
        buf, n = fields[f][1:]
        fields_ready(f)
        for xg in FACE_ORDER:
            z_copy(buf, n, e, xg).start()
        for i in range(4):
            x_post(buf, n, e, chunk_at(i))

    first_post(0, 0)
    fields_ready(1)
    lateral(fwd, 1)

    def tile_copy(i, h):
        other = (quarter + i) % 4
        return pltpu.make_async_remote_copy(
            src_ref=vpiece.at[pl.ds(4 * other, 4), :, part(h)],
            dst_ref=vtile[h].at[slab],
            send_sem=t_send.at[i - 1, h],
            recv_sem=t_recv.at[i - 1, h],
            device_id={"ap": ap_of(half, other)},
            device_id_type=MESH,
        )

    turned = [crossed(table[2 * shots + 4 * quarter + ky]) for ky in range(4)]
    def at_slab(j, ky):
        return j + turned[ky] * (1 - 2 * (j % 2))

    lane_block = lax.broadcasted_iota(jnp.int32, (8, 128), 1) // 32

    for h in range(PARTS):
        lanes_h = slice(WIDE * h, WIDE * h + WIDE)

        @pl.loop(0, shots)
        def _(s):
            @pl.when(s != me)
            def _():
                arrival(vsend, vrecv, s, h, v_send, v_recv).wait_recv()

        @pl.loop(0, 16)
        def _(k):
            vpiece[k, :, lanes_h] = vrecv[h][table[2 * shots + k]]

        for i in range(1, 4):
            tile_copy(i, h).start()
        vtile[h][slab] = vpiece[pl.ds(4 * quarter, 4), :, lanes_h]

    for h in range(PARTS):
        for i in range(1, 4):
            tile_copy(i, h).wait_recv()

        @pl.loop(0, 4)
        def _(j):
            for a in range(BLOCKS * h, BLOCKS * h + BLOCKS):
                tiles = [
                    vtile[h][at_slab(j, ky), ky, :, 128 * (a % BLOCKS) : 128 * (a % BLOCKS) + 128]
                    for ky in range(4)
                ]
                for b in range(4):
                    joined = None
                    for ky in range(4):
                        shift = (32 * (ky - b)) % 128
                        moved = pltpu.roll(tiles[ky], shift, 1) if shift else tiles[ky]
                        joined = (
                            moved if joined is None else jnp.where(lane_block == ky, moved, joined)
                        )
                    turn[8 * (4 * a + b) : 8 * (4 * a + b) + 8, :] = joined
            for z in range(8):
                for x in range(4 * BLOCKS * h, 4 * BLOCKS * h + 4 * BLOCKS, 8):
                    coef[8 * j + z, x : x + 8, :] = turn[pl.ds(8 * x + z, 8, stride=8), :]

    source = table[3 * shots + 16]
    source_z = source // 16384 - 32 * half
    source_x = (source // 128) % 128 - 32 * quarter
    source_in = (source_z >= 0) & (source_z < 32) & (source_x >= 0) & (source_x < 32)
    source_at = jnp.where(source_in, (source_z * 32 + source_x) * 128 + source % 128, -1)
    spot = (
        lax.broadcasted_iota(jnp.int32, (4, 8, 128), 0) * 4096
        + lax.broadcasted_iota(jnp.int32, (4, 8, 128), 1) * 128
        + lax.broadcasted_iota(jnp.int32, (4, 8, 128), 2)
    )

    def laplacian(buf, n, z, xg):
        row = 8 + 8 * xg
        column = buf[n, pl.ds(z, 12), row : row + 8, :]
        total = lap[pl.ds(z, 4), 8 * xg : 8 * xg + 8, :]
        for k in range(1, 5):
            beside = column[4 + k : 8 + k] + column[4 - k : 8 - k]
            beside = beside + (
                buf[n, pl.ds(z + 4, 4), row + k : row + k + 8, :]
                + buf[n, pl.ds(z + 4, 4), row - k : row - k + 8, :]
            )
            total = total + COEF[k] * beside
        return column[4:8], total

    def ahead(n, z, xg):
        at = (pl.ds(z, 4), slice(8 * xg, 8 * xg + 8), slice(None))
        inner = (pl.ds(z + 4, 4), slice(8 + 8 * xg, 16 + 8 * xg), slice(None))
        here, total = laplacian(fwd, n + 1, z, xg)
        fired = jnp.where(spot == source_at - (z * 4096 + xg * 1024), wav[0, n], 0.0)
        speed = coef[at]
        change = (STEP_SQUARE * speed * speed) * (total + fired)
        upd[(n,) + at] = change
        new = 2.0 * here - fwd[(n,) + inner] + change
        fwd[(n + 2,) + inner] = new
        inj[(n,) + at] = count[at] * new - inj[(n,) + at]

    def back(t, z, xg):
        n = 5 - t
        at = (pl.ds(z, 4), slice(8 * xg, 8 * xg + 8), slice(None))
        inner = (pl.ds(z + 4, 4), slice(8 + 8 * xg, 16 + 8 * xg), slice(None))
        here, total = laplacian(adj, n + 1, z, xg)
        speed = coef[at]
        new = (
            2.0 * here
            - adj[(n + 2,) + inner]
            + (STEP_SQUARE * speed * speed) * (total + inj[(n,) + at])
        )
        adj[(n,) + inner] = new
        image[at] = image[at] + new * upd[(n,) + at]

    def group_at(i):
        return 4 * (i * half + (7 - i) * (1 - half))

    def march(buf, unit, t, now, new, e):
        more = t < STEPS - 1

        @pl.loop(1, 8)
        def _(i):
            for xg in (1, 2):
                unit(t, group_at(i), xg)

        for xg in FACE_ORDER:
            if xg == 0:
                x_take(buf, now, e, chunk_at(0))
            z_copy(buf, now, e, xg).wait_recv()
            unit(t, group_at(0), xg)

            @pl.when(more)
            def _():
                z_copy(buf, new, e + 1, xg).start()

        for xg in (0, 3):
            unit(t, group_at(1), xg)

        @pl.when(more)
        def _():
            x_post(buf, new, e + 1, chunk_at(0))

        @pl.loop(1, 4)
        def _(i):
            x_take(buf, now, e, chunk_at(i))
            for g in range(2):
                for xg in (0, 3):
                    unit(t, group_at(2 * i + g), xg)

            @pl.when(more)
            def _():
                x_post(buf, new, e + 1, chunk_at(i))

        @pl.when(more)
        def _():
            lateral(buf, new)

    @pl.loop(0, STEPS)
    def _(t):
        march(fwd, ahead, t, t + 1, t + 2, t)

        @pl.when(t == 3)
        def _():
            first_post(2, 6)

    fields_ready(3)
    lateral(adj, 6)
    image[...] = jnp.zeros(image.shape, F32)

    @pl.loop(0, STEPS)
    def _(t):
        march(adj, back, t, 6 - t, 5 - t, 6 + t)

    @pl.loop(0, 8)
    def _(g):
        at = pl.ds(4 * g, 4)
        turn[pl.ds(128 * g, 128), :] = (image[at] / coef[at]).reshape(128, 128)

    def piece_copy(i, h):
        other = (slab + i) % 4
        return pltpu.make_async_remote_copy(
            src_ref=gtile.at[other, :, :, part(h)],
            dst_ref=gpiece[h].at[pl.ds(4 * quarter, 4)],
            send_sem=p_send.at[i - 1, h],
            recv_sem=p_recv.at[i - 1, h],
            device_id={"ap": 4 * half + other},
            device_id_type=MESH,
        )

    for h in range(PARTS):
        lanes_h = slice(WIDE * h, WIDE * h + WIDE)

        @pl.loop(0, 4)
        def _(j):
            for a in range(BLOCKS * h, BLOCKS * h + BLOCKS):
                for ky in range(4):
                    base = 256 * at_slab(j, ky) + 4 * a
                    rows = [turn[pl.ds(base + b, 8, stride=32), :] for b in range(4)]
                    joined = None
                    for b in range(4):
                        shift = (32 * (b - ky)) % 128
                        moved = pltpu.roll(rows[b], shift, 1) if shift else rows[b]
                        joined = (
                            moved if joined is None else jnp.where(lane_block == b, moved, joined)
                        )
                    gtile[j, ky, :, 128 * a : 128 * a + 128] = joined

        for i in range(1, 4):
            piece_copy(i, h).start()
        gpiece[h][pl.ds(4 * quarter, 4)] = gtile[slab, :, :, lanes_h]

    for h in range(PARTS):
        lanes_h = slice(WIDE * h, WIDE * h + WIDE)
        for i in range(1, 4):
            piece_copy(i, h).wait_recv()

        @pl.loop(0, shots)
        def _(s):
            gsend[s, :, lanes_h] = gpiece[h][table[2 * shots + 16 + s]]

        grecv[h][me] = gpiece[h][table[2 * shots + 16 + me]]
        for core in range(2):
            exchange_start(gsend, grecv, core, h, g_send, g_recv)

    out[...] = jnp.zeros(out.shape, F32)
    planes = shots // 4

    def nearer(m):
        away = planes // 2 - ((m + 1) // 2) * (2 * (m % 2) - 1)
        return 4 * ((me // 4 + planes - away) % planes)

    for h in range(PARTS):

        @pl.loop(0, shots // 8)
        def _(b):
            origins = [nearer(2 * b + i // 4) + i % 4 for i in range(8)]
            for s in origins:

                @pl.when(s != me)
                def _():
                    arrival(gsend, grecv, s, h, g_send, g_recv).wait_recv()

            local = [table[shots + s] for s in origins]

            for a in range(BLOCKS * h, BLOCKS * h + BLOCKS):
                at = (slice(None), slice(128 * a, 128 * a + 128))
                here = (slice(None), slice(128 * (a % BLOCKS), 128 * (a % BLOCKS) + 128))
                parts = [grecv[h][(s,) + here] for s in origins]
                for tile in range(16):
                    total = out[(tile,) + at]
                    for i in range(8):
                        total = total + jnp.where(local[i] == tile, 1.0, 0.0) * parts[i]
                    out[(tile,) + at] = total

    for f in range(4):
        for i in range(1, 4):
            field_copy(f, i).wait_send()

    @pl.loop(0, shots)
    def _(s):
        @pl.when(s != me)
        def _():
            for h in range(PARTS):
                arrival(vsend, vrecv, s, h, v_send, v_recv).wait_send()
                arrival(gsend, grecv, s, h, g_send, g_recv).wait_send()

    for h in range(PARTS):
        for i in range(1, 4):
            tile_copy(i, h).wait_send()
            piece_copy(i, h).wait_send()

    @pl.loop(0, 2 * STEPS)
    def _(e):
        for xg in range(4):
            z_copy(fwd, 1, e, xg).wait_send()

        @pl.loop(0, 4)
        def _(c):
            @pl.when(has_low)
            def _():
                x_copy(e, 0, c).wait_send()

            @pl.when(has_high)
            def _():
                x_copy(e, 1, c).wait_send()


def on_device(
    velocity_tiles,
    aperture_tiles,
    source_cells,
    wavelet,
    receiver_cells,
    observed,
    field_early,
    field_late,
    adjoint_late,
    adjoint_later,
):
    shots = lax.axis_size("shot")
    me = lax.axis_index("shot")
    tiles_dev = velocity_tiles.shape[0]
    owners = aperture_tiles // tiles_dev
    matched = owners == me
    local = jnp.sum(jnp.where(matched, aperture_tiles % tiles_dev, 0), axis=1)
    local_or_none = jnp.where(jnp.any(matched, axis=1), local, -1)
    row = lax.broadcasted_iota(jnp.int32, owners.shape, 0)
    mine = jnp.sum(jnp.where(row == me, owners, 0), axis=0)
    position = jnp.sum(
        jnp.where(mine[None, :] == row, lax.broadcasted_iota(jnp.int32, owners.shape, 1), 0), axis=1
    )

    vmem = pl.BlockSpec(memory_space=pltpu.VMEM)
    smem = pl.BlockSpec(memory_space=pltpu.SMEM)
    anywhere = pl.BlockSpec(memory_space=pl.ANY)
    block = (32, 32, 128)
    dma = pltpu.SemaphoreType.DMA
    half_gradient = pl.pallas_call(
        kernel,
        out_shape=jax.ShapeDtypeStruct(velocity_tiles.shape, F32),
        in_specs=[smem, smem, vmem, anywhere, anywhere, anywhere, anywhere, anywhere, anywhere],
        out_specs=vmem,
        scratch_shapes=[
            pltpu.VMEM((8, 40, 48, 128), F32),
            pltpu.VMEM((8, 40, 48, 128), F32),
            pltpu.VMEM((STEPS,) + block, F32),
            pltpu.VMEM((STEPS,) + block, F32),
            pltpu.VMEM(block, F32),
            pltpu.VMEM(block, F32),
            pltpu.VMEM(block, F32),
            pltpu.VMEM(block, F32),
            pltpu.VMEM((1024, 128), F32),
            pltpu.VMEM((256, 256), BF16),
            pltpu.VMEM((1024, 256), BF16),
            pltpu.VMEM((2 * STEPS, 2, 32, 4, 128), F32),
            pltpu.VMEM((2 * STEPS, 2, 32, 4, 128), F32),
            pltpu.VMEM((shots, 8, 1024), F32),
            (pltpu.VMEM((shots, 8, WIDE), F32),) * PARTS,
            pltpu.VMEM((16, 8, 1024), F32),
            (pltpu.VMEM((4, 4, 8, WIDE), F32),) * PARTS,
            pltpu.VMEM((4, 4, 8, 1024), F32),
            (pltpu.VMEM((16, 8, WIDE), F32),) * PARTS,
            pltpu.VMEM((shots, 8, 1024), F32),
            (pltpu.VMEM((shots, 8, WIDE), F32),) * PARTS,
            pltpu.VMEM((16, 8, 1024), F32),
            pltpu.VMEM((STEPS, 256), F32),
            dma((2,)),
            dma((4, 3)),
            dma((4, 3)),
            dma((4,)),
            dma((2 * STEPS, 4)),
            dma((2 * STEPS, 4)),
            dma((2 * STEPS, 2, 4)),
            dma((2 * STEPS, 2, 4)),
            dma((shots, PARTS)),
            dma((shots, PARTS)),
            dma((shots, PARTS)),
            dma((shots, PARTS)),
            dma((3, PARTS)),
            dma((3, PARTS)),
            dma((3, PARTS)),
            dma((3, PARTS)),
        ],
        compiler_params=pltpu.CompilerParams(
            collective_id=0, has_side_effects=True, vmem_limit_bytes=60 * 1024 * 1024
        ),
        name="inversion",
    )(
        jnp.concatenate([local, local_or_none, mine, position, source_cells]),
        wavelet,
        receiver_cells,
        observed,
        velocity_tiles,
        field_early,
        field_late,
        adjoint_late,
        adjoint_later,
    )
    return 2.0 * half_gradient


def solution(mesh):
    placed = (
        P("shot", "ap", None),
        P(),
        P("shot"),
        P("shot", None),
        P("shot", None),
        P("shot", None, None),
        P("shot", "ap", None, None),
        P("shot", "ap", None, None),
        P("shot", "ap", None, None),
        P("shot", "ap", None, None),
    )
    return jax.shard_map(
        on_device, mesh=mesh, in_specs=placed, out_specs=P("shot", "ap", None), check_vma=False
    )
```

```python
import functools

import jax
import jax.numpy as jnp
from jax import lax
from jax.experimental import pallas as pl
from jax.experimental.pallas import tpu as pltpu
from jax.sharding import PartitionSpec as P

COEF = (-205.0 / 72.0, 8.0 / 5.0, -1.0 / 5.0, 8.0 / 315.0, -1.0 / 560.0)
STEP_SQUARE = 0.01
MESH = pl.DeviceIdType.MESH
STEPS = 6
F32 = jnp.float32
BF16 = jnp.bfloat16
PARTS = 2
VEL_CUTS = (0, 6, 8)
GRAD_CUTS = (0, 2, 8)
FACE_ORDER = (1, 2, 0, 3)
Z_ORDER = (4, 3, 5, 2, 6, 1, 7, 0)


def ap_of(half, quarter):
    mirror = quarter // 2
    y = ((quarter + 1) // 2) % 2
    x = mirror + half * (1 - 2 * mirror)
    return 4 * half + 2 * x + y


def split(value):
    high = value.astype(BF16)
    return high, (value - high.astype(F32)).astype(BF16)


def part(cuts, h):
    return pl.ds(128 * cuts[h], 128 * (cuts[h + 1] - cuts[h]))


def blocks(cuts, h):
    return range(cuts[h], cuts[h + 1])


def kernel(
    table, source_cell, wav, cells, observed, vel_at, early, late, a_late, a_later, out,
    fwd, adj, upd, inj, coef, count, image, lap, turn, ymat, hot,
    xs, xr, vsend, vrecv, vpiece, vtile, gtile, gpiece, gsend, grecv, vel,
    i_sem, f_send, f_recv, f_loc, z_send, z_recv, x_send, x_recv,
    v_send, v_recv, g_send, g_recv, t_send, t_recv, p_send, p_recv,
):
    shots = lax.axis_size("shot")
    me = lax.axis_index("shot")
    ap = lax.axis_index("ap")
    half = ap // 4
    slab = ap % 4
    xl = slab // 2
    yl = slab % 2
    mirror = xl + half * (1 - 2 * xl)
    quarter = yl + mirror * (3 - 2 * yl)
    has_low = quarter > 0
    has_high = quarter < 3

    fields = ((late, fwd, 1), (early, fwd, 0), (a_late, adj, 6), (a_later, adj, 7))

    def own_copy(f):
        source, buf, n = fields[f]
        return pltpu.make_async_copy(
            source.at[0, :, pl.ds(32 * quarter, 32), :],
            buf.at[n, pl.ds(4 + 8 * slab, 8), pl.ds(8, 32), :],
            f_loc.at[f],
        )

    def field_copy(f, i):
        source, buf, n = fields[f]
        other = (quarter + i) % 4
        return pltpu.make_async_remote_copy(
            src_ref=source.at[0, :, pl.ds(32 * other, 32), :],
            dst_ref=buf.at[n, pl.ds(4 + 8 * slab, 8), pl.ds(8, 32), :],
            send_sem=f_send.at[f, i - 1],
            recv_sem=f_recv.at[f, i - 1],
            device_id={"ap": ap_of(half, other)},
            device_id_type=MESH,
        )

    vel_copy = pltpu.make_async_copy(vel_at, vel, i_sem.at[0])
    vel_copy.start()
    barrier = pltpu.get_barrier_semaphore()

    side = (me // 2) % 2
    beside = ap + 1 - 2 * (ap % 2)

    def crossed(shot):
        return (shot // 2 + side) % 2

    @pl.loop(1, shots)
    def _(d):
        other = (me + d) % shots
        pl.semaphore_signal(
            barrier,
            inc=1,
            device_id={"shot": other, "ap": ap + (beside - ap) * crossed(other)},
            device_id_type=MESH,
        )

    for i in range(1, 4):
        pl.semaphore_signal(
            barrier, inc=1, device_id={"ap": ap_of(half, (quarter + i) % 4)}, device_id_type=MESH
        )
    partner = ap_of(1 - half, quarter)
    pl.semaphore_signal(barrier, inc=1, device_id={"ap": partner}, device_id_type=MESH)

    for f in range(4):
        own_copy(f).start()
    vel_copy.wait()

    @pl.loop(0, shots)
    def _(s):
        vsend[s] = vel[table[0, s]]

    for h in range(PARTS):
        vrecv[h][me] = vel[table[0, me], :, part(VEL_CUTS, h)]

    pl.semaphore_wait(barrier, shots - 1 + 4)

    for f in (0, 1):
        for i in range(1, 4):
            field_copy(f, i).start()

    def cuts_of(src):
        return VEL_CUTS if src is vsend else GRAD_CUTS

    def exchange_copy(src, dst, target, cross, h, send, recv):
        return pltpu.make_async_remote_copy(
            src_ref=src.at[target, :, part(cuts_of(src), h)],
            dst_ref=dst[h].at[me],
            send_sem=send.at[target, h],
            recv_sem=recv.at[me, h],
            device_id={"shot": target, "ap": beside if cross else ap},
            device_id_type=MESH,
        )

    def arrival(src, dst, origin, h, send, recv):
        return pltpu.make_async_remote_copy(
            src_ref=src.at[origin, :, part(cuts_of(src), h)],
            dst_ref=dst[h].at[origin],
            send_sem=send.at[origin, h],
            recv_sem=recv.at[origin, h],
            device_id={"shot": origin},
            device_id_type=MESH,
        )

    def exchange_start(src, dst, core, h, send, recv):
        planes = shots // 4
        for dz in range(planes):
            for dy in range(2):
                step = Z_ORDER[dz] if planes == 8 else dz
                target = ((me // 4 + step) % planes) * 4 + ((me // 2 + dy) % 2) * 2 + core

                @pl.when(target != me)
                def _():
                    exchange_copy(src, dst, target, dy, h, send, recv).start()

    for h in range(PARTS):
        for core in range(2):
            exchange_start(vsend, vrecv, core, h, v_send, v_recv)

    for f in (2, 3):
        for i in range(1, 4):
            field_copy(f, i).start()

    distance = jnp.abs(
        lax.broadcasted_iota(jnp.int32, (128, 128), 0)
        - lax.broadcasted_iota(jnp.int32, (128, 128), 1)
    )
    band = jnp.where(distance == 0, 3.0 * COEF[0], 0.0)
    for k in range(1, 5):
        band = jnp.where(distance == k, COEF[k], band)
    band_high, band_low = split(band)
    ymat[0:128, 0:128] = band_high
    ymat[128:256, 0:128] = band_high
    ymat[0:128, 128:256] = band_low
    ymat[128:256, 128:256] = jnp.zeros((128, 128), BF16)

    @pl.loop(1, 7)
    def _(n):
        for buf in (fwd, adj):
            buf[n, pl.ds(36 * half, 4), 8:40, :] = jnp.zeros((4, 32, 128), F32)

        @pl.loop(0, 8)
        def _(g):
            for buf in (fwd, adj):
                buf[n, pl.ds(4 + 4 * g, 4), 0:8, :] = jnp.zeros((4, 8, 128), F32)
                buf[n, pl.ds(4 + 4 * g, 4), 40:48, :] = jnp.zeros((4, 8, 128), F32)

    flat = cells[0:1, :]
    z_at = flat // 16384 - 32 * half
    x_at = (flat // 128) % 128 - 32 * quarter
    y_at = flat % 128
    inside = (z_at >= 0) & (z_at < 32) & (x_at >= 0) & (x_at < 32)
    row_at = jnp.where(inside, z_at * 32 + x_at, -1)
    nrec = cells.shape[1]

    @pl.loop(0, 16)
    def _(b):
        rows = lax.broadcasted_iota(jnp.int32, (64, nrec), 0) + b * 64
        hot[pl.ds(b * 64, 64), :] = jnp.where(rows == row_at, 1.0, 0.0).astype(BF16)

    lanes = jnp.where(
        lax.broadcasted_iota(jnp.int32, (128, nrec), 0) == y_at, 1.0, 0.0
    )
    contract = (((1,), (1,)), ((), ()))
    lanes_low = lanes.astype(BF16)

    @pl.loop(0, 4)
    def _(b):
        found = lax.dot_general(
            hot[pl.ds(b * 256, 256), :], lanes_low, contract, preferred_element_type=F32
        )
        count[pl.ds(8 * b, 8), :, :] = found.reshape(8, 32, 128)

    for n in range(STEPS):
        high, low = split(lanes * observed[0:1, nrec * n : nrec * n + nrec])
        both = jnp.concatenate([high, low], axis=0)

        @pl.loop(0, 4)
        def _(b):
            found = lax.dot_general(
                hot[pl.ds(b * 256, 256), :], both, contract, preferred_element_type=F32
            )
            inj[n, pl.ds(8 * b, 8), :, :] = (found[:, 0:128] + found[:, 128:256]).reshape(
                8, 32, 128
            )

    def z_copy(buf, n, e, xg):
        return pltpu.make_async_remote_copy(
            src_ref=buf.at[n, pl.ds(32 - 28 * half, 4), pl.ds(8 + 8 * xg, 8), :],
            dst_ref=buf.at[n, pl.ds(36 * half, 4), pl.ds(8 + 8 * xg, 8), :],
            send_sem=z_send.at[e, xg],
            recv_sem=z_recv.at[e, xg],
            device_id={"ap": partner},
            device_id_type=MESH,
        )

    def x_copy(e, side, c):
        other = ap_of(half, quarter + (2 * side - 1))
        return pltpu.make_async_remote_copy(
            src_ref=xs.at[e, side, pl.ds(8 * c, 8)],
            dst_ref=xr.at[e, 1 - side, pl.ds(8 * c, 8)],
            send_sem=x_send.at[e, side, c],
            recv_sem=x_recv.at[e, 1 - side, c],
            device_id={"ap": other},
            device_id_type=MESH,
        )

    def x_arrival(e, side, c):
        other = ap_of(half, quarter + (2 * side - 1))
        return pltpu.make_async_remote_copy(
            src_ref=xs.at[e, side, pl.ds(8 * c, 8)],
            dst_ref=xr.at[e, side, pl.ds(8 * c, 8)],
            send_sem=x_send.at[e, side, c],
            recv_sem=x_recv.at[e, side, c],
            device_id={"ap": other},
            device_id_type=MESH,
        )

    def x_post(buf, n, e, c):
        at = pl.ds(4 + 8 * c, 8)

        @pl.when(has_low)
        def _():
            xs[e, 0, pl.ds(8 * c, 8)] = buf[n, at, 8:12, :]
            x_copy(e, 0, c).start()

        @pl.when(has_high)
        def _():
            xs[e, 1, pl.ds(8 * c, 8)] = buf[n, at, 36:40, :]
            x_copy(e, 1, c).start()

    def x_take(buf, n, e, c):
        at = pl.ds(4 + 8 * c, 8)

        @pl.when(has_low)
        def _():
            x_arrival(e, 0, c).wait_recv()
            buf[n, at, 4:8, :] = xr[e, 0, pl.ds(8 * c, 8)]

        @pl.when(has_high)
        def _():
            x_arrival(e, 1, c).wait_recv()
            buf[n, at, 40:44, :] = xr[e, 1, pl.ds(8 * c, 8)]

    def chunk_at(i):
        return i * half + (3 - i) * (1 - half)

    def fields_ready(f):
        own_copy(f).wait()
        for i in range(1, 4):
            field_copy(f, i).wait_recv()

    def lateral(buf, n):
        @pl.loop(0, 4)
        def _(c):
            here = buf[n, pl.ds(4 + 8 * c, 8), 8:40, :].reshape(256, 128)
            both = jnp.concatenate(split(here), axis=1)
            found = jnp.dot(both, ymat[...], preferred_element_type=F32)
            lap[pl.ds(8 * c, 8), :, :] = (found[:, 0:128] + found[:, 128:256]).reshape(8, 32, 128)

    def first_post(f, e):
        buf, n = fields[f][1:]
        fields_ready(f)
        for xg in FACE_ORDER:
            z_copy(buf, n, e, xg).start()
        for i in range(4):
            x_post(buf, n, e, chunk_at(i))

    first_post(0, 0)
    fields_ready(1)
    lateral(fwd, 1)

    def tile_copy(i, h):
        other = (quarter + i) % 4
        return pltpu.make_async_remote_copy(
            src_ref=vpiece.at[pl.ds(4 * other, 4), :, part(VEL_CUTS, h)],
            dst_ref=vtile[h].at[slab],
            send_sem=t_send.at[i - 1, h],
            recv_sem=t_recv.at[i - 1, h],
            device_id={"ap": ap_of(half, other)},
            device_id_type=MESH,
        )

    turned = [crossed(table[3, 4 * quarter + ky]) for ky in range(4)]
    def at_slab(j, ky):
        return j + turned[ky] * (1 - 2 * (j % 2))

    lane_block = lax.broadcasted_iota(jnp.int32, (8, 128), 1) // 32

    for h in range(PARTS):
        lanes_h = part(VEL_CUTS, h)

        @pl.loop(0, shots)
        def _(s):
            @pl.when(s != me)
            def _():
                arrival(vsend, vrecv, s, h, v_send, v_recv).wait_recv()

        @pl.loop(0, 16)
        def _(k):
            vpiece[k, :, lanes_h] = vrecv[h][table[3, k]]

        for i in range(1, 4):
            tile_copy(i, h).start()
        vtile[h][slab] = vpiece[pl.ds(4 * quarter, 4), :, lanes_h]

    for h in range(PARTS):
        for i in range(1, 4):
            tile_copy(i, h).wait_recv()

        @pl.loop(0, 4)
        def _(j):
            for a in blocks(VEL_CUTS, h):
                tiles = [
                    vtile[h][at_slab(j, ky), ky, :, 128 * (a - VEL_CUTS[h]) : 128 * (a - VEL_CUTS[h]) + 128]
                    for ky in range(4)
                ]
                for b in range(4):
                    joined = None
                    for ky in range(4):
                        shift = (32 * (ky - b)) % 128
                        moved = pltpu.roll(tiles[ky], shift, 1) if shift else tiles[ky]
                        joined = (
                            moved if joined is None else jnp.where(lane_block == ky, moved, joined)
                        )
                    turn[8 * (4 * a + b) : 8 * (4 * a + b) + 8, :] = joined
            for z in range(8):
                for x in range(4 * VEL_CUTS[h], 4 * VEL_CUTS[h + 1], 8):
                    coef[8 * j + z, x : x + 8, :] = turn[pl.ds(8 * x + z, 8, stride=8), :]

    source = source_cell[0]
    source_z = source // 16384 - 32 * half
    source_x = (source // 128) % 128 - 32 * quarter
    source_in = (source_z >= 0) & (source_z < 32) & (source_x >= 0) & (source_x < 32)
    source_at = jnp.where(source_in, (source_z * 32 + source_x) * 128 + source % 128, -1)
    spot = (
        lax.broadcasted_iota(jnp.int32, (4, 8, 128), 0) * 4096
        + lax.broadcasted_iota(jnp.int32, (4, 8, 128), 1) * 128
        + lax.broadcasted_iota(jnp.int32, (4, 8, 128), 2)
    )

    def laplacian(buf, n, z, xg):
        row = 8 + 8 * xg
        column = buf[n, pl.ds(z, 12), row : row + 8, :]
        total = lap[pl.ds(z, 4), 8 * xg : 8 * xg + 8, :]
        for k in range(1, 5):
            beside = column[4 + k : 8 + k] + column[4 - k : 8 - k]
            beside = beside + (
                buf[n, pl.ds(z + 4, 4), row + k : row + k + 8, :]
                + buf[n, pl.ds(z + 4, 4), row - k : row - k + 8, :]
            )
            total = total + COEF[k] * beside
        return column[4:8], total

    def ahead(n, z, xg):
        at = (pl.ds(z, 4), slice(8 * xg, 8 * xg + 8), slice(None))
        inner = (pl.ds(z + 4, 4), slice(8 + 8 * xg, 16 + 8 * xg), slice(None))
        here, total = laplacian(fwd, n + 1, z, xg)
        fired = jnp.where(spot == source_at - (z * 4096 + xg * 1024), wav[0, n], 0.0)
        speed = coef[at]
        change = (STEP_SQUARE * speed * speed) * (total + fired)
        upd[(n,) + at] = change
        new = 2.0 * here - fwd[(n,) + inner] + change
        fwd[(n + 2,) + inner] = new
        inj[(n,) + at] = count[at] * new - inj[(n,) + at]

    def back(t, z, xg):
        n = 5 - t
        at = (pl.ds(z, 4), slice(8 * xg, 8 * xg + 8), slice(None))
        inner = (pl.ds(z + 4, 4), slice(8 + 8 * xg, 16 + 8 * xg), slice(None))
        here, total = laplacian(adj, n + 1, z, xg)
        speed = coef[at]
        new = (
            2.0 * here
            - adj[(n + 2,) + inner]
            + (STEP_SQUARE * speed * speed) * (total + inj[(n,) + at])
        )
        adj[(n,) + inner] = new
        image[at] = image[at] + new * upd[(n,) + at]

    def group_at(i):
        return 4 * (i * half + (7 - i) * (1 - half))

    def march(buf, unit, t, now, new, e):
        more = t < STEPS - 1

        @pl.loop(1, 8)
        def _(i):
            for xg in (1, 2):
                unit(t, group_at(i), xg)

        for xg in FACE_ORDER:
            if xg == 0:
                x_take(buf, now, e, chunk_at(0))
            z_copy(buf, now, e, xg).wait_recv()
            unit(t, group_at(0), xg)

            @pl.when(more)
            def _():
                z_copy(buf, new, e + 1, xg).start()

        for xg in (0, 3):
            unit(t, group_at(1), xg)

        @pl.when(more)
        def _():
            x_post(buf, new, e + 1, chunk_at(0))

        @pl.loop(1, 4)
        def _(i):
            x_take(buf, now, e, chunk_at(i))
            for g in range(2):
                for xg in (0, 3):
                    unit(t, group_at(2 * i + g), xg)

            @pl.when(more)
            def _():
                x_post(buf, new, e + 1, chunk_at(i))

        @pl.when(more)
        def _():
            lateral(buf, new)

    @pl.loop(0, STEPS)
    def _(t):
        march(fwd, ahead, t, t + 1, t + 2, t)

        @pl.when(t == 3)
        def _():
            first_post(2, 6)

    fields_ready(3)
    lateral(adj, 6)
    image[...] = jnp.zeros(image.shape, F32)

    @pl.loop(0, STEPS)
    def _(t):
        march(adj, back, t, 6 - t, 5 - t, 6 + t)

    @pl.loop(0, 8)
    def _(g):
        at = pl.ds(4 * g, 4)
        turn[pl.ds(128 * g, 128), :] = (image[at] / coef[at]).reshape(128, 128)

    def piece_copy(i, h):
        other = (slab + i) % 4
        return pltpu.make_async_remote_copy(
            src_ref=gtile.at[other, :, :, part(GRAD_CUTS, h)],
            dst_ref=gpiece[h].at[pl.ds(4 * quarter, 4)],
            send_sem=p_send.at[i - 1, h],
            recv_sem=p_recv.at[i - 1, h],
            device_id={"ap": 4 * half + other},
            device_id_type=MESH,
        )

    for h in range(PARTS):
        lanes_h = part(GRAD_CUTS, h)

        @pl.loop(0, 4)
        def _(j):
            for a in blocks(GRAD_CUTS, h):
                for ky in range(4):
                    base = 256 * at_slab(j, ky) + 4 * a
                    rows = [turn[pl.ds(base + b, 8, stride=32), :] for b in range(4)]
                    joined = None
                    for b in range(4):
                        shift = (32 * (b - ky)) % 128
                        moved = pltpu.roll(rows[b], shift, 1) if shift else rows[b]
                        joined = (
                            moved if joined is None else jnp.where(lane_block == b, moved, joined)
                        )
                    gtile[j, ky, :, 128 * a : 128 * a + 128] = joined

        for i in range(1, 4):
            piece_copy(i, h).start()
        gpiece[h][pl.ds(4 * quarter, 4)] = gtile[slab, :, :, lanes_h]

    for h in range(PARTS):
        lanes_h = part(GRAD_CUTS, h)
        for i in range(1, 4):
            piece_copy(i, h).wait_recv()

        @pl.loop(0, shots)
        def _(s):
            gsend[s, :, lanes_h] = gpiece[h][table[2, s]]

        grecv[h][me] = gpiece[h][table[2, me]]
        for core in range(2):
            exchange_start(gsend, grecv, core, h, g_send, g_recv)

    out[...] = jnp.zeros(out.shape, F32)
    planes = shots // 4

    def nearer(m):
        away = planes // 2 - ((m + 1) // 2) * (2 * (m % 2) - 1)
        return 4 * ((me // 4 + planes - away) % planes)

    for h in range(PARTS):

        @pl.loop(0, shots // 8)
        def _(b):
            origins = [nearer(2 * b + i // 4) + i % 4 for i in range(8)]
            for s in origins:

                @pl.when(s != me)
                def _():
                    arrival(gsend, grecv, s, h, g_send, g_recv).wait_recv()

            local = [table[1, s] for s in origins]

            for a in blocks(GRAD_CUTS, h):
                at = (slice(None), slice(128 * a, 128 * a + 128))
                here = (slice(None), pl.ds(128 * (a - GRAD_CUTS[h]), 128))
                parts = [grecv[h][(s,) + here] for s in origins]
                for tile in range(16):
                    total = out[(tile,) + at]
                    for i in range(8):
                        total = total + jnp.where(local[i] == tile, 1.0, 0.0) * parts[i]
                    out[(tile,) + at] = total

    for f in range(4):
        for i in range(1, 4):
            field_copy(f, i).wait_send()

    @pl.loop(0, shots)
    def _(s):
        @pl.when(s != me)
        def _():
            for h in range(PARTS):
                arrival(vsend, vrecv, s, h, v_send, v_recv).wait_send()
                arrival(gsend, grecv, s, h, g_send, g_recv).wait_send()

    for h in range(PARTS):
        for i in range(1, 4):
            tile_copy(i, h).wait_send()
            piece_copy(i, h).wait_send()

    @pl.loop(0, 2 * STEPS)
    def _(e):
        for xg in range(4):
            z_copy(fwd, 1, e, xg).wait_send()

        @pl.loop(0, 4)
        def _(c):
            @pl.when(has_low)
            def _():
                x_copy(e, 0, c).wait_send()

            @pl.when(has_high)
            def _():
                x_copy(e, 1, c).wait_send()


def on_device(
    velocity_tiles,
    aperture_tiles,
    source_cells,
    wavelet,
    receiver_cells,
    observed,
    field_early,
    field_late,
    adjoint_late,
    adjoint_later,
):
    shots = lax.axis_size("shot")
    me = lax.axis_index("shot")
    tiles_dev = velocity_tiles.shape[0]
    extent = (4,) + aperture_tiles.shape
    which, row, column = (lax.broadcasted_iota(jnp.int32, extent, d) for d in range(3))
    owners = (aperture_tiles // tiles_dev)[None]
    local = (aperture_tiles % tiles_dev)[None]
    mine = lax.dynamic_slice_in_dim(owners, me, 1, 1)
    taken = jnp.where(owners == me, local + jnp.minimum(which, 1), 0)
    placed = jnp.where(mine == row, column, 0)
    listed = jnp.where(column == row, mine, 0)
    terms = jnp.where(which < 2, taken, jnp.where(which == 2, placed, listed))
    table = jnp.sum(terms, axis=2) - jnp.where(which[:, :, 0] == 1, 1, 0)

    vmem = pl.BlockSpec(memory_space=pltpu.VMEM)
    smem = pl.BlockSpec(memory_space=pltpu.SMEM)
    anywhere = pl.BlockSpec(memory_space=pl.ANY)
    block = (32, 32, 128)
    dma = pltpu.SemaphoreType.DMA
    half_gradient = pl.pallas_call(
        kernel,
        out_shape=jax.ShapeDtypeStruct(velocity_tiles.shape, F32),
        in_specs=[smem, smem, smem, vmem, vmem, anywhere, anywhere, anywhere, anywhere, anywhere],
        out_specs=vmem,
        scratch_shapes=[
            pltpu.VMEM((8, 40, 48, 128), F32),
            pltpu.VMEM((8, 40, 48, 128), F32),
            pltpu.VMEM((STEPS,) + block, F32),
            pltpu.VMEM((STEPS,) + block, F32),
            pltpu.VMEM(block, F32),
            pltpu.VMEM(block, F32),
            pltpu.VMEM(block, F32),
            pltpu.VMEM(block, F32),
            pltpu.VMEM((1024, 128), F32),
            pltpu.VMEM((256, 256), BF16),
            pltpu.VMEM((1024, 256), BF16),
            pltpu.VMEM((2 * STEPS, 2, 32, 4, 128), F32),
            pltpu.VMEM((2 * STEPS, 2, 32, 4, 128), F32),
            pltpu.VMEM((shots, 8, 1024), F32),
            tuple(pltpu.VMEM((shots, 8, 128 * (VEL_CUTS[h + 1] - VEL_CUTS[h])), F32) for h in range(PARTS)),
            pltpu.VMEM((16, 8, 1024), F32),
            tuple(pltpu.VMEM((4, 4, 8, 128 * (VEL_CUTS[h + 1] - VEL_CUTS[h])), F32) for h in range(PARTS)),
            pltpu.VMEM((4, 4, 8, 1024), F32),
            tuple(pltpu.VMEM((16, 8, 128 * (GRAD_CUTS[h + 1] - GRAD_CUTS[h])), F32) for h in range(PARTS)),
            pltpu.VMEM((shots, 8, 1024), F32),
            tuple(pltpu.VMEM((shots, 8, 128 * (GRAD_CUTS[h + 1] - GRAD_CUTS[h])), F32) for h in range(PARTS)),
            pltpu.VMEM((16, 8, 1024), F32),
            dma((1,)),
            dma((4, 3)),
            dma((4, 3)),
            dma((4,)),
            dma((2 * STEPS, 4)),
            dma((2 * STEPS, 4)),
            dma((2 * STEPS, 2, 4)),
            dma((2 * STEPS, 2, 4)),
            dma((shots, PARTS)),
            dma((shots, PARTS)),
            dma((shots, PARTS)),
            dma((shots, PARTS)),
            dma((3, PARTS)),
            dma((3, PARTS)),
            dma((3, PARTS)),
            dma((3, PARTS)),
        ],
        compiler_params=pltpu.CompilerParams(
            collective_id=0, has_side_effects=True, vmem_limit_bytes=60 * 1024 * 1024
        ),
        name="inversion",
    )(
        table,
        source_cells,
        wavelet,
        receiver_cells,
        observed.reshape(1, -1),
        velocity_tiles,
        field_early,
        field_late,
        adjoint_late,
        adjoint_later,
    )
    return 2.0 * half_gradient


def solution(mesh):
    placed = (
        P("shot", "ap", None),
        P(),
        P("shot"),
        P("shot", None),
        P("shot", None),
        P("shot", None, None),
        P("shot", "ap", None, None),
        P("shot", "ap", None, None),
        P("shot", "ap", None, None),
        P("shot", "ap", None, None),
    )
    return jax.shard_map(
        on_device, mesh=mesh, in_specs=placed, out_specs=P("shot", "ap", None), check_vma=False
    )
```

```python
import functools

import jax
import jax.numpy as jnp
from jax import lax
from jax.experimental import pallas as pl
from jax.experimental.pallas import tpu as pltpu
from jax.sharding import PartitionSpec as P

COEF = (-205.0 / 72.0, 8.0 / 5.0, -1.0 / 5.0, 8.0 / 315.0, -1.0 / 560.0)
STEP_SQUARE = 0.01
MESH = pl.DeviceIdType.MESH
STEPS = 6
F32 = jnp.float32
BF16 = jnp.bfloat16
PARTS = 2
VEL_CUTS = (0, 6, 8)
GRAD_CUTS = (0, 3, 8)
FACE_ORDER = (1, 2, 0, 3)
Z_ORDER = (4, 3, 5, 2, 6, 1, 7, 0)


def ap_of(half, quarter):
    mirror = quarter // 2
    y = ((quarter + 1) // 2) % 2
    x = mirror + half * (1 - 2 * mirror)
    return 4 * half + 2 * x + y


def split(value):
    high = value.astype(BF16)
    return high, (value - high.astype(F32)).astype(BF16)


def part(cuts, h):
    return pl.ds(128 * cuts[h], 128 * (cuts[h + 1] - cuts[h]))


def blocks(cuts, h):
    return range(cuts[h], cuts[h + 1])


def kernel(
    table, source_cell, wav, cells, observed, vel_at, early, late, a_late, a_later, out,
    fwd, adj, upd, inj, coef, count, image, lap, turn, ymat, hot,
    xs, xr, vsend, vrecv, vpiece, vtile, gtile, gpiece, gsend, grecv, vel,
    i_sem, f_send, f_recv, f_loc, z_send, z_recv, x_send, x_recv,
    v_send, v_recv, g_send, g_recv, t_send, t_recv, p_send, p_recv,
):
    shots = lax.axis_size("shot")
    me = lax.axis_index("shot")
    ap = lax.axis_index("ap")
    half = ap // 4
    slab = ap % 4
    xl = slab // 2
    yl = slab % 2
    mirror = xl + half * (1 - 2 * xl)
    quarter = yl + mirror * (3 - 2 * yl)
    has_low = quarter > 0
    has_high = quarter < 3

    fields = ((late, fwd, 1), (early, fwd, 0), (a_late, adj, 6), (a_later, adj, 7))

    def own_copy(f):
        source, buf, n = fields[f]
        return pltpu.make_async_copy(
            source.at[0, :, pl.ds(32 * quarter, 32), :],
            buf.at[n, pl.ds(4 + 8 * slab, 8), pl.ds(8, 32), :],
            f_loc.at[f],
        )

    def field_copy(f, i):
        source, buf, n = fields[f]
        other = (quarter + i) % 4
        return pltpu.make_async_remote_copy(
            src_ref=source.at[0, :, pl.ds(32 * other, 32), :],
            dst_ref=buf.at[n, pl.ds(4 + 8 * slab, 8), pl.ds(8, 32), :],
            send_sem=f_send.at[f, i - 1],
            recv_sem=f_recv.at[f, i - 1],
            device_id={"ap": ap_of(half, other)},
            device_id_type=MESH,
        )

    vel_copy = pltpu.make_async_copy(vel_at, vel, i_sem.at[0])
    vel_copy.start()
    barrier = pltpu.get_barrier_semaphore()

    side = (me // 2) % 2
    beside = ap + 1 - 2 * (ap % 2)

    def crossed(shot):
        return (shot // 2 + side) % 2

    @pl.loop(1, shots)
    def _(d):
        other = (me + d) % shots
        pl.semaphore_signal(
            barrier,
            inc=1,
            device_id={"shot": other, "ap": ap + (beside - ap) * crossed(other)},
            device_id_type=MESH,
        )

    for i in range(1, 4):
        pl.semaphore_signal(
            barrier, inc=1, device_id={"ap": ap_of(half, (quarter + i) % 4)}, device_id_type=MESH
        )
    partner = ap_of(1 - half, quarter)
    pl.semaphore_signal(barrier, inc=1, device_id={"ap": partner}, device_id_type=MESH)

    for f in range(4):
        own_copy(f).start()
    vel_copy.wait()

    @pl.loop(0, shots)
    def _(s):
        vsend[s] = vel[table[0, s]]

    for h in range(PARTS):
        vrecv[h][me] = vel[table[0, me], :, part(VEL_CUTS, h)]

    pl.semaphore_wait(barrier, shots - 1 + 4)

    for f in (0, 1):
        for i in range(1, 4):
            field_copy(f, i).start()

    def cuts_of(src):
        return VEL_CUTS if src is vsend else GRAD_CUTS

    def exchange_copy(src, dst, target, cross, h, send, recv):
        return pltpu.make_async_remote_copy(
            src_ref=src.at[target, :, part(cuts_of(src), h)],
            dst_ref=dst[h].at[me],
            send_sem=send.at[target, h],
            recv_sem=recv.at[me, h],
            device_id={"shot": target, "ap": beside if cross else ap},
            device_id_type=MESH,
        )

    def arrival(src, dst, origin, h, send, recv):
        return pltpu.make_async_remote_copy(
            src_ref=src.at[origin, :, part(cuts_of(src), h)],
            dst_ref=dst[h].at[origin],
            send_sem=send.at[origin, h],
            recv_sem=recv.at[origin, h],
            device_id={"shot": origin},
            device_id_type=MESH,
        )

    def exchange_start(src, dst, core, h, send, recv):
        planes = shots // 4
        for dz in range(planes):
            for dy in range(2):
                step = Z_ORDER[dz] if planes == 8 else dz
                target = ((me // 4 + step) % planes) * 4 + ((me // 2 + dy) % 2) * 2 + core

                @pl.when(target != me)
                def _():
                    exchange_copy(src, dst, target, dy, h, send, recv).start()

    for h in range(PARTS):
        for core in range(2):
            exchange_start(vsend, vrecv, core, h, v_send, v_recv)

    for f in (2, 3):
        for i in range(1, 4):
            field_copy(f, i).start()

    distance = jnp.abs(
        lax.broadcasted_iota(jnp.int32, (128, 128), 0)
        - lax.broadcasted_iota(jnp.int32, (128, 128), 1)
    )
    band = jnp.where(distance == 0, 3.0 * COEF[0], 0.0)
    for k in range(1, 5):
        band = jnp.where(distance == k, COEF[k], band)
    band_high, band_low = split(band)
    ymat[0:128, 0:128] = band_high
    ymat[128:256, 0:128] = band_high
    ymat[0:128, 128:256] = band_low
    ymat[128:256, 128:256] = jnp.zeros((128, 128), BF16)

    @pl.loop(1, 7)
    def _(n):
        for buf in (fwd, adj):
            buf[n, pl.ds(36 * half, 4), 8:40, :] = jnp.zeros((4, 32, 128), F32)

        @pl.loop(0, 8)
        def _(g):
            for buf in (fwd, adj):
                buf[n, pl.ds(4 + 4 * g, 4), 0:8, :] = jnp.zeros((4, 8, 128), F32)
                buf[n, pl.ds(4 + 4 * g, 4), 40:48, :] = jnp.zeros((4, 8, 128), F32)

    flat = cells[0:1, :]
    z_at = flat // 16384 - 32 * half
    x_at = (flat // 128) % 128 - 32 * quarter
    y_at = flat % 128
    inside = (z_at >= 0) & (z_at < 32) & (x_at >= 0) & (x_at < 32)
    row_at = jnp.where(inside, z_at * 32 + x_at, -1)
    nrec = cells.shape[1]

    @pl.loop(0, 16)
    def _(b):
        rows = lax.broadcasted_iota(jnp.int32, (64, nrec), 0) + b * 64
        hot[pl.ds(b * 64, 64), :] = jnp.where(rows == row_at, 1.0, 0.0).astype(BF16)

    lanes = jnp.where(
        lax.broadcasted_iota(jnp.int32, (128, nrec), 0) == y_at, 1.0, 0.0
    )
    contract = (((1,), (1,)), ((), ()))
    lanes_low = lanes.astype(BF16)

    @pl.loop(0, 4)
    def _(b):
        found = lax.dot_general(
            hot[pl.ds(b * 256, 256), :], lanes_low, contract, preferred_element_type=F32
        )
        count[pl.ds(8 * b, 8), :, :] = found.reshape(8, 32, 128)

    for n in range(STEPS):
        high, low = split(lanes * observed[0:1, nrec * n : nrec * n + nrec])
        both = jnp.concatenate([high, low], axis=0)

        @pl.loop(0, 4)
        def _(b):
            found = lax.dot_general(
                hot[pl.ds(b * 256, 256), :], both, contract, preferred_element_type=F32
            )
            inj[n, pl.ds(8 * b, 8), :, :] = (found[:, 0:128] + found[:, 128:256]).reshape(
                8, 32, 128
            )

    def z_copy(buf, n, e, xg):
        return pltpu.make_async_remote_copy(
            src_ref=buf.at[n, pl.ds(32 - 28 * half, 4), pl.ds(8 + 8 * xg, 8), :],
            dst_ref=buf.at[n, pl.ds(36 * half, 4), pl.ds(8 + 8 * xg, 8), :],
            send_sem=z_send.at[e, xg],
            recv_sem=z_recv.at[e, xg],
            device_id={"ap": partner},
            device_id_type=MESH,
        )

    def x_copy(e, side, c):
        other = ap_of(half, quarter + (2 * side - 1))
        return pltpu.make_async_remote_copy(
            src_ref=xs.at[e, side, pl.ds(8 * c, 8)],
            dst_ref=xr.at[e, 1 - side, pl.ds(8 * c, 8)],
            send_sem=x_send.at[e, side, c],
            recv_sem=x_recv.at[e, 1 - side, c],
            device_id={"ap": other},
            device_id_type=MESH,
        )

    def x_arrival(e, side, c):
        other = ap_of(half, quarter + (2 * side - 1))
        return pltpu.make_async_remote_copy(
            src_ref=xs.at[e, side, pl.ds(8 * c, 8)],
            dst_ref=xr.at[e, side, pl.ds(8 * c, 8)],
            send_sem=x_send.at[e, side, c],
            recv_sem=x_recv.at[e, side, c],
            device_id={"ap": other},
            device_id_type=MESH,
        )

    def x_post(buf, n, e, c):
        at = pl.ds(4 + 8 * c, 8)

        @pl.when(has_low)
        def _():
            xs[e, 0, pl.ds(8 * c, 8)] = buf[n, at, 8:12, :]
            x_copy(e, 0, c).start()

        @pl.when(has_high)
        def _():
            xs[e, 1, pl.ds(8 * c, 8)] = buf[n, at, 36:40, :]
            x_copy(e, 1, c).start()

    def x_take(buf, n, e, c):
        at = pl.ds(4 + 8 * c, 8)

        @pl.when(has_low)
        def _():
            x_arrival(e, 0, c).wait_recv()
            buf[n, at, 4:8, :] = xr[e, 0, pl.ds(8 * c, 8)]

        @pl.when(has_high)
        def _():
            x_arrival(e, 1, c).wait_recv()
            buf[n, at, 40:44, :] = xr[e, 1, pl.ds(8 * c, 8)]

    def chunk_at(i):
        return i * half + (3 - i) * (1 - half)

    def fields_ready(f):
        own_copy(f).wait()
        for i in range(1, 4):
            field_copy(f, i).wait_recv()

    def lateral(buf, n):
        @pl.loop(0, 4)
        def _(c):
            here = buf[n, pl.ds(4 + 8 * c, 8), 8:40, :].reshape(256, 128)
            both = jnp.concatenate(split(here), axis=1)
            found = jnp.dot(both, ymat[...], preferred_element_type=F32)
            lap[pl.ds(8 * c, 8), :, :] = (found[:, 0:128] + found[:, 128:256]).reshape(8, 32, 128)

    def first_post(f, e):
        buf, n = fields[f][1:]
        fields_ready(f)
        for xg in FACE_ORDER:
            z_copy(buf, n, e, xg).start()
        for i in range(4):
            x_post(buf, n, e, chunk_at(i))

    first_post(0, 0)
    fields_ready(1)
    lateral(fwd, 1)

    def tile_copy(i, h):
        other = (quarter + i) % 4
        return pltpu.make_async_remote_copy(
            src_ref=vpiece.at[pl.ds(4 * other, 4), :, part(VEL_CUTS, h)],
            dst_ref=vtile[h].at[slab],
            send_sem=t_send.at[i - 1, h],
            recv_sem=t_recv.at[i - 1, h],
            device_id={"ap": ap_of(half, other)},
            device_id_type=MESH,
        )

    turned = [crossed(table[3, 4 * quarter + ky]) for ky in range(4)]
    def at_slab(j, ky):
        return j + turned[ky] * (1 - 2 * (j % 2))

    lane_block = lax.broadcasted_iota(jnp.int32, (8, 128), 1) // 32

    for h in range(PARTS):
        lanes_h = part(VEL_CUTS, h)

        @pl.loop(0, shots)
        def _(s):
            @pl.when(s != me)
            def _():
                arrival(vsend, vrecv, s, h, v_send, v_recv).wait_recv()

        @pl.loop(0, 16)
        def _(k):
            vpiece[k, :, lanes_h] = vrecv[h][table[3, k]]

        for i in range(1, 4):
            tile_copy(i, h).start()
        vtile[h][slab] = vpiece[pl.ds(4 * quarter, 4), :, lanes_h]

    for h in range(PARTS):
        for i in range(1, 4):
            tile_copy(i, h).wait_recv()

        @pl.loop(0, 4)
        def _(j):
            for a in blocks(VEL_CUTS, h):
                tiles = [
                    vtile[h][at_slab(j, ky), ky, :, 128 * (a - VEL_CUTS[h]) : 128 * (a - VEL_CUTS[h]) + 128]
                    for ky in range(4)
                ]
                for b in range(4):
                    joined = None
                    for ky in range(4):
                        shift = (32 * (ky - b)) % 128
                        moved = pltpu.roll(tiles[ky], shift, 1) if shift else tiles[ky]
                        joined = (
                            moved if joined is None else jnp.where(lane_block == ky, moved, joined)
                        )
                    turn[8 * (4 * a + b) : 8 * (4 * a + b) + 8, :] = joined
            for z in range(8):
                for x in range(4 * VEL_CUTS[h], 4 * VEL_CUTS[h + 1], 8):
                    coef[8 * j + z, x : x + 8, :] = turn[pl.ds(8 * x + z, 8, stride=8), :]

    source = source_cell[0]
    source_z = source // 16384 - 32 * half
    source_x = (source // 128) % 128 - 32 * quarter
    source_in = (source_z >= 0) & (source_z < 32) & (source_x >= 0) & (source_x < 32)
    source_at = jnp.where(source_in, (source_z * 32 + source_x) * 128 + source % 128, -1)
    spot = (
        lax.broadcasted_iota(jnp.int32, (4, 8, 128), 0) * 4096
        + lax.broadcasted_iota(jnp.int32, (4, 8, 128), 1) * 128
        + lax.broadcasted_iota(jnp.int32, (4, 8, 128), 2)
    )

    def laplacian(buf, n, z, xg):
        row = 8 + 8 * xg
        column = buf[n, pl.ds(z, 12), row : row + 8, :]
        total = lap[pl.ds(z, 4), 8 * xg : 8 * xg + 8, :]
        for k in range(1, 5):
            beside = column[4 + k : 8 + k] + column[4 - k : 8 - k]
            beside = beside + (
                buf[n, pl.ds(z + 4, 4), row + k : row + k + 8, :]
                + buf[n, pl.ds(z + 4, 4), row - k : row - k + 8, :]
            )
            total = total + COEF[k] * beside
        return column[4:8], total

    def ahead(n, z, xg):
        at = (pl.ds(z, 4), slice(8 * xg, 8 * xg + 8), slice(None))
        inner = (pl.ds(z + 4, 4), slice(8 + 8 * xg, 16 + 8 * xg), slice(None))
        here, total = laplacian(fwd, n + 1, z, xg)
        fired = jnp.where(spot == source_at - (z * 4096 + xg * 1024), wav[0, n], 0.0)
        speed = coef[at]
        change = (STEP_SQUARE * speed * speed) * (total + fired)
        upd[(n,) + at] = change
        new = 2.0 * here - fwd[(n,) + inner] + change
        fwd[(n + 2,) + inner] = new
        inj[(n,) + at] = count[at] * new - inj[(n,) + at]

    def back(t, z, xg):
        n = 5 - t
        at = (pl.ds(z, 4), slice(8 * xg, 8 * xg + 8), slice(None))
        inner = (pl.ds(z + 4, 4), slice(8 + 8 * xg, 16 + 8 * xg), slice(None))
        here, total = laplacian(adj, n + 1, z, xg)
        speed = coef[at]
        new = (
            2.0 * here
            - adj[(n + 2,) + inner]
            + (STEP_SQUARE * speed * speed) * (total + inj[(n,) + at])
        )
        adj[(n,) + inner] = new
        image[at] = image[at] + new * upd[(n,) + at]

    def group_at(i):
        return 4 * (i * half + (7 - i) * (1 - half))

    def march(buf, unit, t, now, new, e):
        more = t < STEPS - 1

        @pl.loop(1, 8)
        def _(i):
            for xg in (1, 2):
                unit(t, group_at(i), xg)

        for xg in FACE_ORDER:
            if xg == 0:
                x_take(buf, now, e, chunk_at(0))
            z_copy(buf, now, e, xg).wait_recv()
            unit(t, group_at(0), xg)

            @pl.when(more)
            def _():
                z_copy(buf, new, e + 1, xg).start()

        for xg in (0, 3):
            unit(t, group_at(1), xg)

        @pl.when(more)
        def _():
            x_post(buf, new, e + 1, chunk_at(0))

        @pl.loop(1, 4)
        def _(i):
            x_take(buf, now, e, chunk_at(i))
            for g in range(2):
                for xg in (0, 3):
                    unit(t, group_at(2 * i + g), xg)

            @pl.when(more)
            def _():
                x_post(buf, new, e + 1, chunk_at(i))

        @pl.when(more)
        def _():
            lateral(buf, new)

    @pl.loop(0, STEPS)
    def _(t):
        march(fwd, ahead, t, t + 1, t + 2, t)

        @pl.when(t == 3)
        def _():
            first_post(2, 6)

    fields_ready(3)
    lateral(adj, 6)
    image[...] = jnp.zeros(image.shape, F32)

    @pl.loop(0, STEPS)
    def _(t):
        march(adj, back, t, 6 - t, 5 - t, 6 + t)

    @pl.loop(0, 8)
    def _(g):
        at = pl.ds(4 * g, 4)
        turn[pl.ds(128 * g, 128), :] = (image[at] / coef[at]).reshape(128, 128)

    def piece_copy(i, h):
        other = (slab + i) % 4
        return pltpu.make_async_remote_copy(
            src_ref=gtile.at[other, :, :, part(GRAD_CUTS, h)],
            dst_ref=gpiece[h].at[pl.ds(4 * quarter, 4)],
            send_sem=p_send.at[i - 1, h],
            recv_sem=p_recv.at[i - 1, h],
            device_id={"ap": 4 * half + other},
            device_id_type=MESH,
        )

    for h in range(PARTS):
        lanes_h = part(GRAD_CUTS, h)

        @pl.loop(0, 4)
        def _(j):
            for a in blocks(GRAD_CUTS, h):
                for ky in range(4):
                    base = 256 * at_slab(j, ky) + 4 * a
                    rows = [turn[pl.ds(base + b, 8, stride=32), :] for b in range(4)]
                    joined = None
                    for b in range(4):
                        shift = (32 * (b - ky)) % 128
                        moved = pltpu.roll(rows[b], shift, 1) if shift else rows[b]
                        joined = (
                            moved if joined is None else jnp.where(lane_block == b, moved, joined)
                        )
                    gtile[j, ky, :, 128 * a : 128 * a + 128] = joined

        for i in range(1, 4):
            piece_copy(i, h).start()
        gpiece[h][pl.ds(4 * quarter, 4)] = gtile[slab, :, :, lanes_h]

    for h in range(PARTS):
        lanes_h = part(GRAD_CUTS, h)
        for i in range(1, 4):
            piece_copy(i, h).wait_recv()

        @pl.loop(0, shots)
        def _(s):
            gsend[s, :, lanes_h] = gpiece[h][table[2, s]]

        grecv[h][me] = gpiece[h][table[2, me]]
        for core in range(2):
            exchange_start(gsend, grecv, core, h, g_send, g_recv)

    out[...] = jnp.zeros(out.shape, F32)
    planes = shots // 4

    def nearer(m):
        away = planes // 2 - ((m + 1) // 2) * (2 * (m % 2) - 1)
        return 4 * ((me // 4 + planes - away) % planes)

    for h in range(PARTS):

        @pl.loop(0, shots // 8)
        def _(b):
            origins = [nearer(2 * b + i // 4) + i % 4 for i in range(8)]
            for s in origins:

                @pl.when(s != me)
                def _():
                    arrival(gsend, grecv, s, h, g_send, g_recv).wait_recv()

            local = [table[1, s] for s in origins]

            for a in blocks(GRAD_CUTS, h):
                at = (slice(None), slice(128 * a, 128 * a + 128))
                here = (slice(None), pl.ds(128 * (a - GRAD_CUTS[h]), 128))
                parts = [grecv[h][(s,) + here] for s in origins]
                for tile in range(16):
                    total = out[(tile,) + at]
                    for i in range(8):
                        total = total + jnp.where(local[i] == tile, 1.0, 0.0) * parts[i]
                    out[(tile,) + at] = total

    for f in range(4):
        for i in range(1, 4):
            field_copy(f, i).wait_send()

    @pl.loop(0, shots)
    def _(s):
        @pl.when(s != me)
        def _():
            for h in range(PARTS):
                arrival(vsend, vrecv, s, h, v_send, v_recv).wait_send()
                arrival(gsend, grecv, s, h, g_send, g_recv).wait_send()

    for h in range(PARTS):
        for i in range(1, 4):
            tile_copy(i, h).wait_send()
            piece_copy(i, h).wait_send()

    @pl.loop(0, 2 * STEPS)
    def _(e):
        for xg in range(4):
            z_copy(fwd, 1, e, xg).wait_send()

        @pl.loop(0, 4)
        def _(c):
            @pl.when(has_low)
            def _():
                x_copy(e, 0, c).wait_send()

            @pl.when(has_high)
            def _():
                x_copy(e, 1, c).wait_send()


def on_device(
    velocity_tiles,
    aperture_tiles,
    source_cells,
    wavelet,
    receiver_cells,
    observed,
    field_early,
    field_late,
    adjoint_late,
    adjoint_later,
):
    shots = lax.axis_size("shot")
    me = lax.axis_index("shot")
    tiles_dev = velocity_tiles.shape[0]
    extent = (4,) + aperture_tiles.shape
    which, row, column = (lax.broadcasted_iota(jnp.int32, extent, d) for d in range(3))
    owners = (aperture_tiles // tiles_dev)[None]
    local = (aperture_tiles % tiles_dev)[None]
    mine = lax.dynamic_slice_in_dim(owners, me, 1, 1)
    taken = jnp.where(owners == me, local + jnp.minimum(which, 1), 0)
    placed = jnp.where(mine == row, column, 0)
    listed = jnp.where(column == row, mine, 0)
    terms = jnp.where(which < 2, taken, jnp.where(which == 2, placed, listed))
    table = jnp.sum(terms, axis=2) - jnp.where(which[:, :, 0] == 1, 1, 0)

    vmem = pl.BlockSpec(memory_space=pltpu.VMEM)
    smem = pl.BlockSpec(memory_space=pltpu.SMEM)
    anywhere = pl.BlockSpec(memory_space=pl.ANY)
    block = (32, 32, 128)
    dma = pltpu.SemaphoreType.DMA
    half_gradient = pl.pallas_call(
        kernel,
        out_shape=jax.ShapeDtypeStruct(velocity_tiles.shape, F32),
        in_specs=[smem, smem, smem, vmem, vmem, anywhere, anywhere, anywhere, anywhere, anywhere],
        out_specs=vmem,
        scratch_shapes=[
            pltpu.VMEM((8, 40, 48, 128), F32),
            pltpu.VMEM((8, 40, 48, 128), F32),
            pltpu.VMEM((STEPS,) + block, F32),
            pltpu.VMEM((STEPS,) + block, F32),
            pltpu.VMEM(block, F32),
            pltpu.VMEM(block, F32),
            pltpu.VMEM(block, F32),
            pltpu.VMEM(block, F32),
            pltpu.VMEM((1024, 128), F32),
            pltpu.VMEM((256, 256), BF16),
            pltpu.VMEM((1024, 256), BF16),
            pltpu.VMEM((2 * STEPS, 2, 32, 4, 128), F32),
            pltpu.VMEM((2 * STEPS, 2, 32, 4, 128), F32),
            pltpu.VMEM((shots, 8, 1024), F32),
            tuple(pltpu.VMEM((shots, 8, 128 * (VEL_CUTS[h + 1] - VEL_CUTS[h])), F32) for h in range(PARTS)),
            pltpu.VMEM((16, 8, 1024), F32),
            tuple(pltpu.VMEM((4, 4, 8, 128 * (VEL_CUTS[h + 1] - VEL_CUTS[h])), F32) for h in range(PARTS)),
            pltpu.VMEM((4, 4, 8, 1024), F32),
            tuple(pltpu.VMEM((16, 8, 128 * (GRAD_CUTS[h + 1] - GRAD_CUTS[h])), F32) for h in range(PARTS)),
            pltpu.VMEM((shots, 8, 1024), F32),
            tuple(pltpu.VMEM((shots, 8, 128 * (GRAD_CUTS[h + 1] - GRAD_CUTS[h])), F32) for h in range(PARTS)),
            pltpu.VMEM((16, 8, 1024), F32),
            dma((1,)),
            dma((4, 3)),
            dma((4, 3)),
            dma((4,)),
            dma((2 * STEPS, 4)),
            dma((2 * STEPS, 4)),
            dma((2 * STEPS, 2, 4)),
            dma((2 * STEPS, 2, 4)),
            dma((shots, PARTS)),
            dma((shots, PARTS)),
            dma((shots, PARTS)),
            dma((shots, PARTS)),
            dma((3, PARTS)),
            dma((3, PARTS)),
            dma((3, PARTS)),
            dma((3, PARTS)),
        ],
        compiler_params=pltpu.CompilerParams(
            collective_id=0, has_side_effects=True, vmem_limit_bytes=60 * 1024 * 1024
        ),
        name="inversion",
    )(
        table,
        source_cells,
        wavelet,
        receiver_cells,
        observed.reshape(1, -1),
        velocity_tiles,
        field_early,
        field_late,
        adjoint_late,
        adjoint_later,
    )
    return 2.0 * half_gradient


def solution(mesh):
    placed = (
        P("shot", "ap", None),
        P(),
        P("shot"),
        P("shot", None),
        P("shot", None),
        P("shot", None, None),
        P("shot", "ap", None, None),
        P("shot", "ap", None, None),
        P("shot", "ap", None, None),
        P("shot", "ap", None, None),
    )
    return jax.shard_map(
        on_device, mesh=mesh, in_specs=placed, out_specs=P("shot", "ap", None), check_vma=False
    )
```
